32 devices in a mesh: rows: 8 (over z, y), heads: 4 (over x, core).
Axes of the slice: x: 2, y: 2, z: 4, core: 2. Of those that a mesh axis runs over, the one named last changes fastest.
Arguments:
- hidden_in: bfloat16 [32768, 768], P(('rows', 'heads')), may hold values from -6 to 6
- cotangent: bfloat16 [32768, 768], P(('rows', 'heads')), may hold values from -6 to 6
- part_lengths: int32 [32, 2], P('rows'), may hold values from 1 to 512, as said below
- segment_start: int32 [32], P('rows'), may hold values from 1 to 1023, as said below
- query_weight: bfloat16 [768, 768], replicated, may hold values from -0.21875 to 0.21875
- value_weight: bfloat16 [768, 768], replicated, may hold values from -0.21875 to 0.21875
- shared_down: bfloat16 [768, 1024], replicated, may hold values from -0.21875 to 0.21875
- shared_up: bfloat16 [1024, 768], replicated, may hold values from -0.1875 to 0.1875
- owner: int32 [640], replicated, may hold values from 0 to 31, as said below
- weights: float32 [15360, 768], P(('rows', 'heads'))
- first_moment: float32 [15360, 768], P(('rows', 'heads'))
- second_moment: float32 [15360, 768], P(('rows', 'heads')), as said below
- small_weights: float32 [11264], P(('rows', 'heads'))
- small_first: float32 [11264], P(('rows', 'heads'))
- small_second: float32 [11264], P(('rows', 'heads')), as said below
Outputs:
- block_out: bfloat16 [32768, 768], P(('rows', 'heads'))
- input_grad: bfloat16 [32768, 768], P(('rows', 'heads'))
- new_weights: float32 [15360, 768], P(('rows', 'heads'))
- new_first: float32 [15360, 768], P(('rows', 'heads'))
- new_second: float32 [15360, 768], P(('rows', 'heads'))
- weights_copy: bfloat16 [15360, 768], P(('rows', 'heads'))
- new_small: float32 [11264], P(('rows', 'heads'))
- new_small_first: float32 [11264], P(('rows', 'heads'))
- new_small_second: float32 [11264], P(('rows', 'heads'))
- small_copy: bfloat16 [11264], P(('rows', 'heads'))
The draws below stay inside these ranges and needn't reach their ends.
Inputs may be any that keep to these rules, and one draw needn't show every extreme that they name: Part one holds positions 0 to part_lengths[s, 0] - 1; some sequence has a part of exactly 512 tokens. part_lengths[s, 0] <= segment_start[s] and segment_start[s] + part_lengths[s, 1] <= 1024; other positions are padding. `owner`: no device owns more than 40 blocks, and some device owns exactly 40. `second_moment`: entries are positive. `small_second`: entries are positive.
All inputs are finite; a program needn't handle non-finite values.
Results may differ from the reference program's by a relative error of at most 0.015.
The reference program's roundings to bfloat16 on the way count: a program that leaves them out, or rounds other values in their place, can miss the bound.
Values may be sent and summed in bfloat16 or wider, within the bound.
No kernel may reach another device: no remote copies, remote signals or barrier semaphores. Data moves between devices by JAX's collectives and lax.ppermute only.
A program may use at most 256 MiB of HBM per device.

```python
import math
import jax
import jax.numpy as jnp
from jax import lax

D = 768
FF = 3072
HEAD_COUNT = 12
HEAD_DIM = 64
RANK = 1024
SEQ_LEN = 1024
STEP = 3
BLOCK_ROWS = 12
SEQS_GRP = 4
SEQS = 32
TOKENS = 32768
NB = 640
CAP = 40
SLOT_ROWS = 15360
SMALLN = 11264
N_ROWS = 8
DEVICES = 32


def slot_index_drawn(owner, capacity):
    count = owner.shape[0]
    order = jnp.arange(count, dtype=jnp.int32)
    same_owner = owner[:, None] == owner[None, :]
    earlier = order[None, :] < order[:, None]
    ranked = jnp.sum((same_owner & earlier).astype(jnp.int32), axis=1)
    return (owner * capacity + ranked).astype(jnp.int32)


def owner_law(key):
    slot_count = DEVICES * CAP
    first_key, second_key = jax.random.split(jax.random.fold_in(key, 11))
    heavy = jax.random.randint(first_key, (), 0, DEVICES)
    ranking = jax.random.permutation(second_key, slot_count).astype(jnp.int32)
    places = jnp.arange(slot_count, dtype=jnp.int32)
    scoring = jnp.where(places // CAP == heavy, places - slot_count, ranking)
    scoring = jnp.where(places == 0, -2 * slot_count - 2, scoring)
    scoring = jnp.where(places == slot_count - 1, -2 * slot_count - 1, scoring)
    chosen = jnp.argsort(scoring)[:NB]
    return (chosen // CAP).astype(jnp.int32)


def draw_owner(key, part):
    return owner_law(key)


def pair_law(key):
    key_a, key_b, key_c, key_d = jax.random.split(jax.random.fold_in(key, 31), 4)
    half = SEQ_LEN // 2
    first_len = jax.random.randint(key_a, (SEQS,), 1, half + 1)
    second_len = jax.random.randint(key_b, (SEQS,), 1, half + 1)
    picked = jax.random.permutation(key_c, SEQS)
    first_len = jnp.where(picked == 0, half, first_len)
    second_len = jnp.where(picked == 1, half, second_len)
    first_len = jnp.where(picked == 2, 1, first_len)
    second_len = jnp.where(picked == 3, 1, second_len)
    room = SEQ_LEN - first_len - second_len
    spacing = jax.random.randint(key_d, (SEQS,), 0, room + 1)
    spacing = jnp.where(picked == 2, 0, spacing)
    spacing = jnp.where(picked == 3, room, spacing)
    starts = first_len + spacing
    return (jnp.stack([first_len, second_len], axis=1).astype(jnp.int32), starts.astype(jnp.int32))


def draw_part_lengths(key, part):
    return pair_law(key)[0]


def draw_segment_start(key, part):
    return pair_law(key)[1]


def row_factor(key, kinds, empty):
    owner = owner_law(key)
    slot = slot_index_drawn(owner, CAP)
    per_row = jnp.concatenate([jnp.full((count,), value, jnp.float32) for count, value in zip([D, D, FF, FF], kinds)])
    per_block = per_row.reshape(NB, BLOCK_ROWS)
    slot_count = DEVICES * CAP
    match = slot[None, :] == jnp.arange(slot_count, dtype=jnp.int32)[:, None]
    source = jnp.sum(match.astype(jnp.int32) * jnp.arange(NB, dtype=jnp.int32)[None, :], axis=1)
    filled = jnp.any(match, axis=1)
    rowed = jnp.where(filled[:, None], per_block[source], empty)
    return rowed.reshape(-1, 1)


def signed_moment(key, shape, scale):
    sign_key, size_key = jax.random.split(key)
    signs = jnp.where(jax.random.bernoulli(sign_key, 0.5, shape), 1.0, -1.0)
    magnitude = jax.random.uniform(size_key, shape, jnp.float32, 0.5, 1.5)
    return (signs * magnitude * scale).astype(jnp.float32)


def square_moment(key, shape, scale):
    factor = jnp.exp(jax.random.uniform(key, shape, jnp.float32, 0.0, math.log(4.0)))
    return (scale * scale * factor).astype(jnp.float32)


def draw_weights(key, part):
    factor = row_factor(key, [D ** (-0.5), (SEQ_LEN / (5.4 * D)) ** 0.5, D ** (-0.5), FF ** (-0.5)], D ** (-0.5))
    noise_key = jax.random.fold_in(key, 21)
    noise = jax.random.normal(noise_key, (SLOT_ROWS, D), jnp.float32)
    return noise * factor


def draw_first_moment(key, part):
    scale = row_factor(key, [0.3, 0.06, 0.25, 0.5], 0.3) * math.sqrt(TOKENS)
    return signed_moment(jax.random.fold_in(key, 22), (SLOT_ROWS, D), scale)


def draw_second_moment(key, part):
    scale = row_factor(key, [0.3, 0.06, 0.25, 0.5], 0.3) * math.sqrt(TOKENS)
    return square_moment(jax.random.fold_in(key, 23), (SLOT_ROWS, D), scale)


def small_table(values):
    counted = [RANK, RANK, D, D, D, FF, D, D, D, D, D]
    return jnp.concatenate([jnp.full((count,), value, jnp.float32) for count, value in zip(counted, values)])


def draw_small_weights(key, part):
    centre = small_table([0.6, 0.6, 0.0, 0.0, 0.0, 0.0, 0.0, 1.0, 0.0, 1.0, 0.0])
    spread = small_table([0.4, 0.4, 0.7, 0.7, 0.3, 0.3, 0.3, 0.3, 0.3, 0.3, 0.3])
    flatness = small_table([1.0, 1.0, 0.0, 0.0, 0.0, 0.0, 0.0, 1.0, 0.0, 1.0, 0.0])
    even_key, bell_key = jax.random.split(jax.random.fold_in(key, 41))
    even = jax.random.uniform(even_key, (SMALLN,), jnp.float32, -1.0, 1.0)
    bell = jax.random.normal(bell_key, (SMALLN,), jnp.float32)
    return centre + spread * (flatness * even + (1.0 - flatness) * bell)


def small_scale():
    return small_table([0.3, 0.3, 0.3, 0.3, 0.7, 0.25, 0.8, 1.0, 1.0, 1.0, 1.0]) * math.sqrt(TOKENS)


def draw_small_first(key, part):
    return signed_moment(jax.random.fold_in(key, 42), (SMALLN,), small_scale())


def draw_small_second(key, part):
    return square_moment(jax.random.fold_in(key, 43), (SMALLN,), small_scale())


def levels(key, shape, cuts, low, top_value):
    def one(position, shards_of):
        draws = jax.random.uniform(jax.random.fold_in(jax.random.fold_in(key, 6), position), (shards_of,), jnp.float32, low / len(cuts), top_value / len(cuts))
        return jnp.repeat(jnp.exp(draws), shape[position] // shards_of).reshape((-1,) + (1,) * (len(shape) - position - 1))

    factor_of = one(*cuts[0])
    for cut in cuts[1:]:
        factor_of = factor_of * one(*cut)
    return factor_of


def bell_draw(stream_key, extent, deviation, limit, cuts=(), kind=jnp.bfloat16):
    level = levels(stream_key, extent, cuts, -0.22, 0.18) if cuts else 1.0
    array = jax.random.normal(stream_key, extent, jnp.float32) * deviation * level
    return jnp.minimum(jnp.maximum(array, -limit), limit).astype(kind)


def setup_inputs(seed: int = 0) -> dict:
    streams_of = jax.random.split(jax.random.key(seed), 16)
    return {
        "hidden_in": bell_draw(streams_of[0], (TOKENS, D), 1.0, 6.0, ((0, 32),)),
        "cotangent": bell_draw(streams_of[1], (TOKENS, D), 1.0, 6.0, ((0, 32),)),
        "part_lengths": draw_part_lengths(jax.random.fold_in(streams_of[15], 71), 0),
        "segment_start": draw_segment_start(jax.random.fold_in(streams_of[15], 71), 0),
        "query_weight": bell_draw(streams_of[4], (D, D), D ** -0.5, 0.21875),
        "value_weight": bell_draw(streams_of[5], (D, D), D ** -0.5, 0.21875),
        "shared_down": bell_draw(streams_of[6], (D, RANK), D ** -0.5, 0.21875),
        "shared_up": bell_draw(streams_of[7], (RANK, D), RANK ** -0.5, 0.1875),
        "owner": draw_owner(jax.random.fold_in(streams_of[15], 71), 0),
        "weights": draw_weights(jax.random.fold_in(streams_of[15], 71), 0),
        "first_moment": draw_first_moment(jax.random.fold_in(streams_of[15], 71), 0),
        "second_moment": draw_second_moment(jax.random.fold_in(streams_of[15], 71), 0),
        "small_weights": draw_small_weights(jax.random.fold_in(streams_of[15], 71), 0),
        "small_first": draw_small_first(jax.random.fold_in(streams_of[15], 71), 0),
        "small_second": draw_small_second(jax.random.fold_in(streams_of[15], 71), 0),
    }


@jax.custom_vjp
def low(v):
    return lax.optimization_barrier(v.astype(jnp.bfloat16)).astype(jnp.float32)

@jax.custom_vjp
def low_back(v):
    return v

def low_keep(v):
    return (low(v), None)

def low_pass(kept, grad):
    return (grad,)

def back_keep(v):
    return (v, None)

def back_low(kept, grad):
    return (low(grad),)
low.defvjp(low_keep, low_pass)
low_back.defvjp(back_keep, back_low)

def matmul(left, right):
    return jnp.dot(left, right, precision=lax.Precision.HIGHEST)

def slot_index(owner, capacity):
    count = owner.shape[0]
    order = jnp.arange(count, dtype=jnp.int32)
    same_owner = owner[:, None] == owner[None, :]
    earlier = order[None, :] < order[:, None]
    ranked = lax.optimization_barrier(jnp.sum((same_owner & earlier).astype(jnp.int32), axis=1))
    return (owner * capacity + ranked).astype(jnp.int32)

def split_small(vector):
    widths = [RANK, RANK, D, D, D, FF, D, D, D, D, D]
    pieces = []
    offset = 0
    for width in widths:
        pieces.append(vector[offset:offset + width])
        offset = offset + width
    return pieces

def visibility(lengths, starts):
    places = jnp.arange(SEQ_LEN, dtype=jnp.int32)[None, :]
    first_len = lengths[:, 0:1]
    second_len = lengths[:, 1:2]
    begin = starts[:, None]
    return (places < first_len) | (places >= begin) & (places < begin + second_len)

def layer_norm(values, gain, shift):
    centre = lax.optimization_barrier(jnp.mean(values, axis=-1, keepdims=True))
    centred = values - centre
    spread = lax.optimization_barrier(jnp.mean(centred * centred, axis=-1, keepdims=True))
    return centred * lax.rsqrt(spread + 1e-05) * gain + shift

def attend_one(pieces):
    query, keys, values, visible = pieces
    scores = low_back(jnp.einsum('qhd,khd->hqk', query, keys, precision=lax.Precision.HIGHEST) * 0.125)
    scores = jnp.where(visible[None, None, :], scores, -1e+30)
    highest = lax.optimization_barrier(jnp.max(scores, axis=-1, keepdims=True))
    raised = jnp.exp(scores - highest)
    probs = raised / lax.optimization_barrier(jnp.sum(raised, axis=-1, keepdims=True))
    return jnp.einsum('hqk,khd->qhd', low(probs), values, precision=lax.Precision.HIGHEST)

def forward(params, inputs, frozen, visible):
    key_rows, out_rows, up_rows, down_rows, small = [low(item) for item in params]
    scale_q_rank, scale_v_rank, scale_q_out, scale_v_out, out_bias, up_bias, down_bias, gain_one, shift_one, gain_two, shift_two = split_small(small)
    query_weight, value_weight, shared_down, shared_up = frozen
    projected = low(low_back(matmul(inputs, shared_down)))
    side_q = low_back(matmul(low(scale_q_rank * projected), shared_up))
    side_v = low_back(matmul(low(scale_v_rank * projected), shared_up))
    query = low(low_back(matmul(inputs, query_weight) + scale_q_out * side_q))
    keys = low(low_back(matmul(inputs, key_rows)))
    values = low(low_back(matmul(inputs, value_weight) + scale_v_out * side_v))
    head_shape = (-1, SEQ_LEN, HEAD_COUNT, HEAD_DIM)
    context = lax.map(jax.checkpoint(attend_one), (query.reshape(head_shape), keys.reshape(head_shape), values.reshape(head_shape), visible))
    context = low(low_back(context.reshape(-1, D)))
    attended = low_back(matmul(context, out_rows) + out_bias)
    hidden_one = layer_norm(inputs + attended, gain_one, shift_one)
    pre_act = low_back(matmul(low(hidden_one), up_rows.T) + up_bias)
    active = low(jax.nn.gelu(pre_act, approximate=False))
    branch = low_back(matmul(active, down_rows) + down_bias)
    return layer_norm(hidden_one + branch, gain_two, shift_two)

def adamw_update(master, first, second, grad, decay, rate):
    correct = 1.0 - 0.5 ** STEP
    first_new = 0.5 * first + 0.5 * grad
    second_new = 0.5 * second + 0.5 * grad * grad
    update = first_new / correct / (jnp.sqrt(second_new / correct) + 1e-08) + decay * master
    return (master - rate * update, first_new, second_new)

def reference(hidden_in, cotangent, part_lengths, segment_start, query_weight, value_weight, shared_down, shared_up, owner, weights, first_moment, second_moment, small_weights, small_first, small_second):
    slot = slot_index(owner, CAP)
    rows = weights.reshape(-1, BLOCK_ROWS, D)[slot].reshape(-1, D)
    params = (rows[:D], rows[D:2 * D], rows[2 * D:2 * D + FF], rows[2 * D + FF:], small_weights)
    frozen = tuple((item.astype(jnp.float32) for item in (query_weight, value_weight, shared_down, shared_up)))
    group_tokens = SEQS_GRP * SEQ_LEN
    inputs = hidden_in.astype(jnp.float32).reshape(N_ROWS, group_tokens, D)
    cotangents = cotangent.astype(jnp.float32).reshape(N_ROWS, group_tokens, D)
    lengths = part_lengths.reshape(N_ROWS, SEQS_GRP, 2)
    starts = segment_start.reshape(N_ROWS, SEQS_GRP)

    def one_group(summed, pieces):
        group_in, group_cot, group_len, group_start = pieces
        visible = visibility(group_len, group_start)

        def run(param_set, layer_in):
            return forward(param_set, layer_in, frozen, visible)
        layer_out, pull = jax.vjp(run, params, group_in)
        param_grad, in_grad = pull(group_cot)
        summed = jax.tree.map(lambda left, right: left + right, summed, param_grad)
        return (summed, (layer_out.astype(jnp.bfloat16), in_grad.astype(jnp.bfloat16)))
    start_sums = jax.tree.map(jnp.zeros_like, params)
    grads, (block_out, input_grad) = lax.scan(one_group, start_sums, (inputs, cotangents, lengths, starts))
    grad_rows = jnp.concatenate(list(grads[:4]), axis=0).reshape(-1, BLOCK_ROWS, D)
    slot_grad = jnp.zeros((DEVICES * CAP, BLOCK_ROWS, D), jnp.float32).at[slot].set(grad_rows).reshape(-1, D)
    new_weights, new_first, new_second = adamw_update(weights, first_moment, second_moment, slot_grad, 0.01, 0.03)
    new_small, new_small_first, new_small_second = adamw_update(small_weights, small_first, small_second, grads[4], 0.0, 0.3)
    return (block_out.reshape(TOKENS, D), input_grad.reshape(TOKENS, D), new_weights, new_first, new_second, new_weights.astype(jnp.bfloat16), new_small, new_small_first, new_small_second, new_small.astype(jnp.bfloat16))
```

```python
import jax
import jax.numpy as jnp
from jax import lax
from jax.experimental import pallas as pl
from jax.experimental.pallas import tpu as pltpu
from jax.sharding import PartitionSpec as P

D = 768
FF = 3072
HEAD_DIM = 64
RANK = 1024
SEQ_LEN = 1024
STEP = 3
BLOCK_ROWS = 12


def slot_index(owner, capacity):
    count = owner.shape[0]
    order = jnp.arange(count, dtype=jnp.int32)
    same_owner = owner[:, None] == owner[None, :]
    earlier = order[None, :] < order[:, None]
    ranked = jnp.sum((same_owner & earlier).astype(jnp.int32), axis=1)
    return owner * capacity + ranked


def split_small(vector):
    widths = [RANK, RANK, D, D, D, FF, D, D, D, D, D]
    pieces = []
    offset = 0
    for width in widths:
        pieces.append(vector[offset : offset + width])
        offset = offset + width
    return pieces


def unpack_rows(gathered, slot):
    rows = gathered.reshape(-1, BLOCK_ROWS, D)[slot].reshape(-1, D)
    return (rows[:D], rows[D : 2 * D], rows[2 * D : 2 * D + FF], rows[2 * D + FF :])


def product(left, right):
    return jnp.dot(left, right, preferred_element_type=jnp.float32)


def product_t(left, right):
    return lax.dot_general(
        left, right, (((1,), (1,)), ((), ())), preferred_element_type=jnp.float32
    )


def inner_rows(left, right):
    return lax.dot_general(
        left, right, (((0,), (0,)), ((), ())), preferred_element_type=jnp.float32
    )


def normalize(values):
    centre = jnp.mean(values, axis=-1, keepdims=True)
    centred = values - centre
    spread = jnp.mean(centred * centred, axis=-1, keepdims=True)
    inverse = lax.rsqrt(spread + 1e-05)
    return (centred * inverse, inverse)


def norm_back(grad_norm, normed, inverse):
    first_mean = jnp.mean(grad_norm, axis=-1, keepdims=True)
    second_mean = jnp.mean(grad_norm * normed, axis=-1, keepdims=True)
    return inverse * (grad_norm - first_mean - normed * second_mean)


PAIR = 2 * HEAD_DIM
TILE = 256


def lane_split(rows):
    return lax.broadcasted_iota(jnp.int32, (rows, PAIR), 1)


def visible_bias(spans, rows):
    place = lax.broadcasted_iota(jnp.int32, (rows, PAIR), 0)
    first_end = spans[0]
    begin = spans[2]
    seen = (place < first_end) | ((place >= begin) & (place < begin + spans[1]))
    return jnp.where(seen, 0.0, -1e30)


def score_operands(query, keys, bias, lanes, half):
    mine = (lanes < HEAD_DIM) == (half == 0)
    spare = lanes == (HEAD_DIM if half == 0 else 0)
    query_h = jnp.where(mine, query * 0.125, jnp.where(spare, 1.0, 0.0)).astype(jnp.bfloat16)
    keys_h = jnp.where(mine, keys, bias).astype(jnp.bfloat16)
    return (mine, query_h, keys_h)


def attend_forward_kernel(spans, query_ref, keys_ref, values_ref, context_ref, total_ref, turned):
    rows = query_ref.shape[0]
    lanes = lane_split(rows)
    bias = visible_bias(spans, rows)
    query = query_ref[...].astype(jnp.float32)
    keys = keys_ref[...].astype(jnp.float32)
    values_t = values_ref[...].astype(jnp.float32).T
    feature = lax.broadcasted_iota(jnp.int32, values_t.shape, 0)
    for half in range(2):
        _, query_h, keys_h = score_operands(query, keys, bias, lanes, half)
        own = (feature < HEAD_DIM) == (half == 0)
        values_h = jnp.where(own, values_t, 1.0).astype(jnp.bfloat16)
        low = half * HEAD_DIM
        other = HEAD_DIM - low
        for start in range(0, rows, TILE):
            scores = product_t(keys_h, query_h[start : start + TILE])
            highest = jnp.max(scores, axis=0, keepdims=True)
            raised = jnp.exp(scores - highest).astype(jnp.bfloat16)
            mixed = product(values_h, raised)
            summed = mixed[other : other + 1]
            total_ref[0, half : half + 1, start : start + TILE] = highest + jnp.log(summed)
            turned[low : low + HEAD_DIM, start : start + TILE] = (
                mixed[low : low + HEAD_DIM] / summed
            )
    context_ref[...] = turned[...].T.astype(jnp.bfloat16)


def attend_backward_kernel(
    spans,
    query_ref,
    keys_ref,
    values_ref,
    context_ref,
    grad_ref,
    total_ref,
    grad_query_ref,
    grad_keys_ref,
    grad_values_ref,
    turned,
    keys_sum,
    values_sum,
):
    rows = query_ref.shape[0]
    lanes = lane_split(rows)
    bias = visible_bias(spans, rows)
    query = query_ref[...].astype(jnp.float32)
    keys = keys_ref[...].astype(jnp.float32)
    values = values_ref[...].astype(jnp.float32)
    grad = grad_ref[...].astype(jnp.float32)
    dots = (grad * context_ref[...].astype(jnp.float32)).T
    keys_t = keys.T
    feature = lax.broadcasted_iota(jnp.int32, keys_t.shape, 0)
    grad_low = grad_ref[...]
    for half in range(2):
        mine, query_h, keys_h = score_operands(query, keys, bias, lanes, half)
        values_h = jnp.where(mine, values, 0.0).astype(jnp.bfloat16)
        grad_h = jnp.where(mine, grad, 0.0).astype(jnp.bfloat16)
        query_m = jnp.where(mine, query * 0.125, 0.0).astype(jnp.bfloat16)
        own = (feature < HEAD_DIM) == (half == 0)
        keys_th = jnp.where(own, keys_t * 0.125, 0.0).astype(jnp.bfloat16)
        low = half * HEAD_DIM
        row_dot = jnp.sum(dots[low : low + HEAD_DIM], axis=0, keepdims=True)
        for start in range(0, rows, TILE):
            part = slice(start, start + TILE)
            scores = product_t(keys_h, query_h[part])
            probs = jnp.exp(scores - total_ref[0, half : half + 1, part])
            grad_probs = product_t(values_h, grad_low[part])
            grad_scores = (probs * (grad_probs - row_dot[:, part])).astype(jnp.bfloat16)
            values_part = product(probs.astype(jnp.bfloat16), grad_h[part])
            keys_part = product(grad_scores, query_m[part])
            query_part = product(keys_th, grad_scores)
            if half == 0 and start == 0:
                values_sum[...] = values_part
                keys_sum[...] = keys_part
            else:
                values_sum[...] += values_part
                keys_sum[...] += keys_part
            if half == 0:
                turned[:, part] = query_part
            else:
                turned[:, part] += query_part
    grad_query_ref[...] = turned[...].T.astype(jnp.bfloat16)
    grad_keys_ref[...] = keys_sum[...].astype(jnp.bfloat16)
    grad_values_ref[...] = values_sum[...].astype(jnp.bfloat16)


def pair_specs(rows):
    wide = pl.BlockSpec((rows, PAIR), lambda i, spans: (0, i))
    total = pl.BlockSpec((1, 2, rows), lambda i, spans: (i, 0, 0))
    return (wide, total)


def attend_forward(spans, query, keys, values):
    rows, width = query.shape
    pairs = width // PAIR
    wide, total = pair_specs(rows)
    return pl.pallas_call(
        attend_forward_kernel,
        out_shape=(
            jax.ShapeDtypeStruct((rows, width), jnp.bfloat16),
            jax.ShapeDtypeStruct((pairs, 2, rows), jnp.float32),
        ),
        grid_spec=pltpu.PrefetchScalarGridSpec(
            num_scalar_prefetch=1,
            grid=(pairs,),
            in_specs=[wide, wide, wide],
            out_specs=(wide, total),
            scratch_shapes=[pltpu.VMEM((PAIR, rows), jnp.float32)],
        ),
        name="attend_forward",
    )(spans, query, keys, values)


def attend_backward(spans, query, keys, values, context, grad_context, log_total):
    rows, width = query.shape
    pairs = width // PAIR
    wide, total = pair_specs(rows)
    shape = jax.ShapeDtypeStruct((rows, width), jnp.bfloat16)
    return pl.pallas_call(
        attend_backward_kernel,
        out_shape=(shape, shape, shape),
        grid_spec=pltpu.PrefetchScalarGridSpec(
            num_scalar_prefetch=1,
            grid=(pairs,),
            in_specs=[wide, wide, wide, wide, wide, total],
            out_specs=(wide, wide, wide),
            scratch_shapes=[
                pltpu.VMEM((PAIR, rows), jnp.float32),
                pltpu.VMEM((rows, PAIR), jnp.float32),
                pltpu.VMEM((rows, PAIR), jnp.float32),
            ],
        ),
        name="attend_backward",
    )(spans, query, keys, values, context, grad_context, log_total)


AXES = ("rows", "heads")


def exchange(values, bit, devices):
    return lax.ppermute(values, AXES, [(i, i ^ bit) for i in range(devices)])


def my_bit(bit):
    return (lax.axis_index(AXES) & bit) != 0


def gather_small(values, devices):
    rows = values[None, :]
    bit = 1
    while bit < devices:
        other = exchange(rows, bit, devices)
        rows = jnp.where(
            my_bit(bit),
            jnp.concatenate([other, rows], axis=0),
            jnp.concatenate([rows, other], axis=0),
        )
        bit = bit * 2
    return rows.reshape(-1)


def reduce_halves(values, devices):
    bit = 1
    while bit < devices:
        half = values.shape[0] // 2
        upper = my_bit(bit)
        low_part = values[:half]
        high_part = values[half:]
        keep = jnp.where(upper, high_part, low_part).astype(jnp.float32)
        sent = jnp.where(upper, low_part, high_part)
        values = (keep + exchange(sent, bit, devices).astype(jnp.float32)).astype(values.dtype)
        bit = bit * 2
    return values


def reverse_bits(count):
    width = count.bit_length() - 1
    return [int(format(i, "b").zfill(width)[::-1], 2) for i in range(count)]


def all_to_all(values):
    return lax.all_to_all(values, AXES, split_axis=0, concat_axis=0, tiled=True)


def pieces_of(rows, devices):
    return rows.reshape(-1, devices, BLOCK_ROWS * D // devices).transpose(1, 0, 2)


def rows_of(pieces):
    return pieces.transpose(1, 0, 2).reshape(-1, D)


def route_in(rows, place, slots, devices):
    pieces = all_to_all(pieces_of(rows, devices)).reshape(slots, -1)
    chosen = place[:, None] == jnp.arange(slots, dtype=jnp.int32)[None, :]
    homed = product(chosen.astype(jnp.bfloat16), pieces).astype(jnp.bfloat16)
    return rows_of(all_to_all(homed.reshape(devices, -1, pieces.shape[1])))


def route_out(rows, place, slots, devices):
    pieces = all_to_all(pieces_of(rows, devices)).reshape(place.shape[0], -1)
    chosen = place[:, None] == jnp.arange(slots, dtype=jnp.int32)[None, :]
    slotted = inner_rows(chosen.astype(jnp.bfloat16), pieces).astype(jnp.bfloat16)
    return rows_of(all_to_all(slotted.reshape(devices, -1, pieces.shape[1])))


def gather_rows(weights, slot, devices):
    blocks = slot.shape[0]
    slots = devices * (weights.shape[0] // BLOCK_ROWS)
    low = weights.astype(jnp.bfloat16)
    if blocks % devices == 0 and (BLOCK_ROWS * D) % devices == 0:
        homed = route_in(low, slot, slots, devices)
        rows = lax.all_gather(homed, AXES, axis=0, tiled=True)
        return (rows[:D], rows[D : 2 * D], rows[2 * D : 2 * D + FF], rows[2 * D + FF :])
    return unpack_rows(lax.all_gather(low, AXES, axis=0, tiled=True), slot)


def scatter_grads(grad_key, grad_rest, small_grad, slot, slots, devices):
    key_blocks = D // BLOCK_ROWS
    blocks = slot.shape[0]
    share = small_grad.shape[0] // devices
    if key_blocks % devices or (blocks - key_blocks) % devices or share > D:
        rows = jnp.concatenate([grad_key, *grad_rest], axis=0).reshape(blocks, BLOCK_ROWS * D)
        chosen = slot[:, None] == jnp.arange(slots, dtype=jnp.int32)[None, :]
        slotted = inner_rows(chosen.astype(jnp.bfloat16), rows).astype(jnp.bfloat16)
        return (
            lax.psum_scatter(slotted.reshape(-1, D), AXES, scatter_dimension=0, tiled=True),
            lax.psum_scatter(small_grad, AXES, scatter_dimension=0, tiled=True),
        )
    rest = jnp.concatenate(grad_rest, axis=0)
    rest_home = lax.psum_scatter(rest, AXES, scatter_dimension=0, tiled=True)
    order = jnp.array(reverse_bits(devices), dtype=jnp.int32)
    key_rows = D // devices
    wide = -(-(key_rows + 1) // 16) * 16
    small_rows = small_grad.reshape(devices, share)[order].astype(jnp.bfloat16)
    small_rows = jnp.pad(small_rows[:, None, :], ((0, 0), (0, wide - key_rows - 1), (0, D - share)))
    packed = jnp.concatenate([grad_key.reshape(devices, key_rows, D), small_rows], axis=1)
    summed = reduce_halves(packed.reshape(-1, D), devices)
    home = jnp.concatenate([summed[:key_rows], rest_home], axis=0)
    place = jnp.concatenate(
        [
            slot[:key_blocks].reshape(devices, -1)[order],
            slot[key_blocks:].reshape(devices, -1),
        ],
        axis=1,
    ).reshape(-1)
    return (
        route_out(home, place, slots, devices).astype(jnp.float32),
        summed[key_rows, :share].astype(jnp.float32),
    )


def adamw_update(master, first, second, grad, decay, rate):
    correct = 1.0 - 0.5**STEP
    first_new = 0.5 * first + 0.5 * grad
    second_new = 0.5 * second + 0.5 * grad * grad
    update = first_new / correct / (jnp.sqrt(second_new / correct) + 1e-08) + decay * master
    return (master - rate * update, first_new, second_new)


def body(
    hidden_in,
    cotangent,
    part_lengths,
    segment_start,
    query_weight,
    value_weight,
    shared_down,
    shared_up,
    owner,
    weights,
    first_moment,
    second_moment,
    small_weights,
    small_first,
    small_second,
):
    capacity = weights.shape[0] // BLOCK_ROWS
    devices = lax.axis_size("rows") * lax.axis_size("heads")
    slot = slot_index(owner, capacity)
    small_all = gather_small(small_weights.astype(jnp.bfloat16), devices)
    key_rows, out_rows, up_rows, down_rows = gather_rows(weights, slot, devices)
    (
        scale_q_rank,
        scale_v_rank,
        scale_q_out,
        scale_v_out,
        out_bias,
        up_bias,
        down_bias,
        gain_one,
        shift_one,
        gain_two,
        shift_two,
    ) = [piece.astype(jnp.float32) for piece in split_small(small_all)]
    projected = product(hidden_in, shared_down).astype(jnp.bfloat16)
    projected_wide = projected.astype(jnp.float32)
    rank_q = (scale_q_rank * projected_wide).astype(jnp.bfloat16)
    rank_v = (scale_v_rank * projected_wide).astype(jnp.bfloat16)
    side_q = product(rank_q, shared_up)
    side_v = product(rank_v, shared_up)
    query = (product(hidden_in, query_weight) + scale_q_out * side_q).astype(jnp.bfloat16)
    keys = product(hidden_in, key_rows).astype(jnp.bfloat16)
    values = (product(hidden_in, value_weight) + scale_v_out * side_v).astype(jnp.bfloat16)
    mine = lax.axis_index("heads")
    spans = jnp.concatenate([part_lengths[mine], segment_start[mine][None]])
    context, log_total = attend_forward(spans, query, keys, values)
    attended = product(context, out_rows) + out_bias
    first_sum = hidden_in.astype(jnp.float32) + attended
    norm_one, inverse_one = normalize(first_sum)
    hidden_one = norm_one * gain_one + shift_one
    hidden_low = hidden_one.astype(jnp.bfloat16)
    pre_act = product_t(hidden_low, up_rows) + up_bias
    share = 0.5 * (1.0 + lax.erf(pre_act * 0.7071067811865476))
    slope = share + pre_act * jnp.exp(-0.5 * pre_act * pre_act) * 0.3989422804014327
    active, slope = lax.optimization_barrier(
        ((pre_act * share).astype(jnp.bfloat16), slope.astype(jnp.bfloat16))
    )
    second_sum = hidden_one + product(active, down_rows) + down_bias
    norm_two, inverse_two = normalize(second_sum)
    block_out = (norm_two * gain_two + shift_two).astype(jnp.bfloat16)
    grad_top = cotangent.astype(jnp.float32)
    grad_gain_two = jnp.sum(grad_top * norm_two, axis=0)
    grad_shift_two = jnp.sum(grad_top, axis=0)
    grad_second = norm_back(grad_top * gain_two, norm_two, inverse_two)
    grad_branch = grad_second.astype(jnp.bfloat16)
    grad_down_bias = jnp.sum(grad_branch.astype(jnp.float32), axis=0)
    grad_down = inner_rows(active, grad_branch).astype(jnp.bfloat16)
    grad_pre = (product_t(grad_branch, down_rows) * slope.astype(jnp.float32)).astype(jnp.bfloat16)
    grad_up_bias = jnp.sum(grad_pre.astype(jnp.float32), axis=0)
    grad_up = inner_rows(grad_pre, hidden_low).astype(jnp.bfloat16)
    grad_hidden = grad_second + product(grad_pre, up_rows)
    grad_gain_one = jnp.sum(grad_hidden * norm_one, axis=0)
    grad_shift_one = jnp.sum(grad_hidden, axis=0)
    grad_first = norm_back(grad_hidden * gain_one, norm_one, inverse_one)
    grad_attended = grad_first.astype(jnp.bfloat16)
    grad_out_bias = jnp.sum(grad_attended.astype(jnp.float32), axis=0)
    grad_out = inner_rows(context, grad_attended).astype(jnp.bfloat16)
    grad_context = product_t(grad_attended, out_rows).astype(jnp.bfloat16)
    grad_query, grad_keys, grad_values = attend_backward(
        spans, query, keys, values, context, grad_context, log_total
    )
    grad_key = inner_rows(hidden_in, grad_keys).astype(jnp.bfloat16)
    grad_query_wide = grad_query.astype(jnp.float32)
    grad_values_wide = grad_values.astype(jnp.float32)
    grad_scale_q_out = jnp.sum(grad_query_wide * side_q, axis=0)
    grad_scale_v_out = jnp.sum(grad_values_wide * side_v, axis=0)
    grad_side_q = (scale_q_out * grad_query_wide).astype(jnp.bfloat16)
    grad_side_v = (scale_v_out * grad_values_wide).astype(jnp.bfloat16)
    grad_rank_q = product_t(grad_side_q, shared_up)
    grad_rank_v = product_t(grad_side_v, shared_up)
    grad_scale_q_rank = jnp.sum(grad_rank_q * projected_wide, axis=0)
    grad_scale_v_rank = jnp.sum(grad_rank_v * projected_wide, axis=0)
    grad_projected = (grad_rank_q * scale_q_rank + grad_rank_v * scale_v_rank).astype(jnp.bfloat16)
    grad_input = grad_first + product_t(grad_query, query_weight) + product_t(grad_keys, key_rows)
    grad_input = (
        grad_input + product_t(grad_values, value_weight) + product_t(grad_projected, shared_down)
    )
    input_grad = grad_input.astype(jnp.bfloat16)
    small_grad = jnp.concatenate(
        [
            grad_scale_q_rank,
            grad_scale_v_rank,
            grad_scale_q_out,
            grad_scale_v_out,
            grad_out_bias,
            grad_up_bias,
            grad_down_bias,
            grad_gain_one,
            grad_shift_one,
            grad_gain_two,
            grad_shift_two,
        ]
    )
    owned_grad, owned_small = scatter_grads(
        grad_key, (grad_out, grad_up, grad_down), small_grad, slot, devices * capacity, devices
    )
    new_weights, new_first, new_second = adamw_update(
        weights, first_moment, second_moment, owned_grad, 0.01, 0.03
    )
    new_small, new_small_first, new_small_second = adamw_update(
        small_weights, small_first, small_second, owned_small, 0.0, 0.3
    )
    return (
        block_out,
        input_grad,
        new_weights,
        new_first,
        new_second,
        new_weights.astype(jnp.bfloat16),
        new_small,
        new_small_first,
        new_small_second,
        new_small.astype(jnp.bfloat16),
    )


def solution(mesh):
    return jax.shard_map(
        body,
        mesh=mesh,
        in_specs=(
            P(("rows", "heads"), None),
            P(("rows", "heads"), None),
            P("rows", None),
            P("rows"),
            P(),
            P(),
            P(),
            P(),
            P(),
            P(("rows", "heads"), None),
            P(("rows", "heads"), None),
            P(("rows", "heads"), None),
            P(("rows", "heads")),
            P(("rows", "heads")),
            P(("rows", "heads")),
        ),
        out_specs=(
            P(("rows", "heads"), None),
            P(("rows", "heads"), None),
            P(("rows", "heads"), None),
            P(("rows", "heads"), None),
            P(("rows", "heads"), None),
            P(("rows", "heads"), None),
            P(("rows", "heads")),
            P(("rows", "heads")),
            P(("rows", "heads")),
            P(("rows", "heads")),
        ),
        check_vma=False,
    )
```

```python
import jax
import jax.numpy as jnp
from jax import lax
from jax.experimental import pallas as pl
from jax.experimental.pallas import tpu as pltpu
from jax.sharding import PartitionSpec as P

D = 768
FF = 3072
HEAD_DIM = 64
RANK = 1024
SEQ_LEN = 1024
STEP = 3
BLOCK_ROWS = 12


def slot_index(owner, capacity):
    count = owner.shape[0]
    order = jnp.arange(count, dtype=jnp.int32)
    same_owner = owner[:, None] == owner[None, :]
    earlier = order[None, :] < order[:, None]
    ranked = jnp.sum((same_owner & earlier).astype(jnp.int32), axis=1)
    return owner * capacity + ranked


def split_small(vector):
    widths = [RANK, RANK, D, D, D, FF, D, D, D, D, D]
    pieces = []
    offset = 0
    for width in widths:
        pieces.append(vector[offset : offset + width])
        offset = offset + width
    return pieces


def unpack_rows(gathered, slot):
    rows = gathered.reshape(-1, BLOCK_ROWS, D)[slot].reshape(-1, D)
    return (rows[:D], rows[D : 2 * D], rows[2 * D : 2 * D + FF], rows[2 * D + FF :])


def product(left, right):
    return jnp.dot(left, right, preferred_element_type=jnp.float32)


def product_t(left, right):
    return lax.dot_general(
        left, right, (((1,), (1,)), ((), ())), preferred_element_type=jnp.float32
    )


def inner_rows(left, right):
    return lax.dot_general(
        left, right, (((0,), (0,)), ((), ())), preferred_element_type=jnp.float32
    )


def normalize(values):
    centre = jnp.mean(values, axis=-1, keepdims=True)
    centred = values - centre
    spread = jnp.mean(centred * centred, axis=-1, keepdims=True)
    inverse = lax.rsqrt(spread + 1e-05)
    return (centred * inverse, inverse)


def norm_back(grad_norm, normed, inverse):
    first_mean = jnp.mean(grad_norm, axis=-1, keepdims=True)
    second_mean = jnp.mean(grad_norm * normed, axis=-1, keepdims=True)
    return inverse * (grad_norm - first_mean - normed * second_mean)


PAIR = 2 * HEAD_DIM
TILE = 256


def lane_split(rows):
    return lax.broadcasted_iota(jnp.int32, (rows, PAIR), 1)


def visible_bias(spans, rows):
    place = lax.broadcasted_iota(jnp.int32, (rows, PAIR), 0)
    first_end = spans[0]
    begin = spans[2]
    seen = (place < first_end) | ((place >= begin) & (place < begin + spans[1]))
    return jnp.where(seen, 0.0, -1e30)


def score_operands(query, keys, bias, lanes, half):
    mine = (lanes < HEAD_DIM) == (half == 0)
    spare = lanes == (HEAD_DIM if half == 0 else 0)
    query_h = jnp.where(mine, query * 0.125, jnp.where(spare, 1.0, 0.0)).astype(jnp.bfloat16)
    keys_h = jnp.where(mine, keys, bias).astype(jnp.bfloat16)
    return (mine, query_h, keys_h)


def attend_forward_kernel(spans, query_ref, keys_ref, values_ref, context_ref, total_ref, turned):
    rows = query_ref.shape[0]
    lanes = lane_split(rows)
    bias = visible_bias(spans, rows)
    query = query_ref[...].astype(jnp.float32)
    keys = keys_ref[...].astype(jnp.float32)
    values_t = values_ref[...].astype(jnp.float32).T
    feature = lax.broadcasted_iota(jnp.int32, values_t.shape, 0)
    operands = []
    for half in range(2):
        _, query_h, keys_h = score_operands(query, keys, bias, lanes, half)
        own = (feature < HEAD_DIM) == (half == 0)
        operands.append((query_h, keys_h, jnp.where(own, values_t, 1.0).astype(jnp.bfloat16)))
    steps = [(half, start) for half in range(2) for start in range(0, rows, TILE)]

    def scores_of(step):
        half, start = step
        return product_t(operands[half][1], operands[half][0][start : start + TILE])

    ready = [scores_of(step) for step in steps[:2]]
    for index, (half, start) in enumerate(steps):
        if index + 2 < len(steps):
            ready.append(scores_of(steps[index + 2]))
        scores = ready.pop(0)
        low = half * HEAD_DIM
        other = HEAD_DIM - low
        highest = jnp.max(scores, axis=0, keepdims=True)
        raised = jnp.exp(scores - highest).astype(jnp.bfloat16)
        mixed = product(operands[half][2], raised)
        summed = mixed[other : other + 1]
        total_ref[0, half : half + 1, start : start + TILE] = highest + jnp.log(summed)
        turned[low : low + HEAD_DIM, start : start + TILE] = mixed[low : low + HEAD_DIM] / summed
    context_ref[...] = turned[...].T.astype(jnp.bfloat16)


def attend_backward_kernel(
    spans,
    query_ref,
    keys_ref,
    values_ref,
    context_ref,
    grad_ref,
    total_ref,
    grad_query_ref,
    grad_keys_ref,
    grad_values_ref,
    turned,
    keys_sum,
    values_sum,
):
    rows = query_ref.shape[0]
    lanes = lane_split(rows)
    bias = visible_bias(spans, rows)
    query = query_ref[...].astype(jnp.float32)
    keys = keys_ref[...].astype(jnp.float32)
    values = values_ref[...].astype(jnp.float32)
    grad = grad_ref[...].astype(jnp.float32)
    dots = (grad * context_ref[...].astype(jnp.float32)).T
    keys_t = keys.T
    feature = lax.broadcasted_iota(jnp.int32, keys_t.shape, 0)
    grad_low = grad_ref[...]
    for half in range(2):
        mine, query_h, keys_h = score_operands(query, keys, bias, lanes, half)
        values_h = jnp.where(mine, values, 0.0).astype(jnp.bfloat16)
        grad_h = jnp.where(mine, grad, 0.0).astype(jnp.bfloat16)
        query_m = jnp.where(mine, query * 0.125, 0.0).astype(jnp.bfloat16)
        own = (feature < HEAD_DIM) == (half == 0)
        keys_th = jnp.where(own, keys_t * 0.125, 0.0).astype(jnp.bfloat16)
        low = half * HEAD_DIM
        row_dot = jnp.sum(dots[low : low + HEAD_DIM], axis=0, keepdims=True)
        for start in range(0, rows, TILE):
            part = slice(start, start + TILE)
            scores = product_t(keys_h, query_h[part])
            probs = jnp.exp(scores - total_ref[0, half : half + 1, part])
            grad_probs = product_t(values_h, grad_low[part])
            grad_scores = (probs * (grad_probs - row_dot[:, part])).astype(jnp.bfloat16)
            values_part = product(probs.astype(jnp.bfloat16), grad_h[part])
            keys_part = product(grad_scores, query_m[part])
            query_part = product(keys_th, grad_scores)
            if half == 0 and start == 0:
                values_sum[...] = values_part
                keys_sum[...] = keys_part
            else:
                values_sum[...] += values_part
                keys_sum[...] += keys_part
            if half == 0:
                turned[:, part] = query_part
            else:
                turned[:, part] += query_part
    grad_query_ref[...] = turned[...].T.astype(jnp.bfloat16)
    grad_keys_ref[...] = keys_sum[...].astype(jnp.bfloat16)
    grad_values_ref[...] = values_sum[...].astype(jnp.bfloat16)


def pair_specs(rows):
    wide = pl.BlockSpec((rows, PAIR), lambda i, spans: (0, i))
    total = pl.BlockSpec((1, 2, rows), lambda i, spans: (i, 0, 0))
    return (wide, total)


def attend_forward(spans, query, keys, values):
    rows, width = query.shape
    pairs = width // PAIR
    wide, total = pair_specs(rows)
    return pl.pallas_call(
        attend_forward_kernel,
        out_shape=(
            jax.ShapeDtypeStruct((rows, width), jnp.bfloat16),
            jax.ShapeDtypeStruct((pairs, 2, rows), jnp.float32),
        ),
        grid_spec=pltpu.PrefetchScalarGridSpec(
            num_scalar_prefetch=1,
            grid=(pairs,),
            in_specs=[wide, wide, wide],
            out_specs=(wide, total),
            scratch_shapes=[pltpu.VMEM((PAIR, rows), jnp.float32)],
        ),
        name="attend_forward",
    )(spans, query, keys, values)


def attend_backward(spans, query, keys, values, context, grad_context, log_total):
    rows, width = query.shape
    pairs = width // PAIR
    wide, total = pair_specs(rows)
    shape = jax.ShapeDtypeStruct((rows, width), jnp.bfloat16)
    return pl.pallas_call(
        attend_backward_kernel,
        out_shape=(shape, shape, shape),
        grid_spec=pltpu.PrefetchScalarGridSpec(
            num_scalar_prefetch=1,
            grid=(pairs,),
            in_specs=[wide, wide, wide, wide, wide, total],
            out_specs=(wide, wide, wide),
            scratch_shapes=[
                pltpu.VMEM((PAIR, rows), jnp.float32),
                pltpu.VMEM((rows, PAIR), jnp.float32),
                pltpu.VMEM((rows, PAIR), jnp.float32),
            ],
        ),
        name="attend_backward",
    )(spans, query, keys, values, context, grad_context, log_total)


AXES = ("rows", "heads")


def exchange(values, bit, devices):
    return lax.ppermute(values, AXES, [(i, i ^ bit) for i in range(devices)])


def my_bit(bit):
    return (lax.axis_index(AXES) & bit) != 0


def gather_doubling(rows, devices):
    bit = devices // 2
    while bit:
        other = exchange(rows, bit, devices)
        upper = my_bit(bit)
        rows = jnp.concatenate(
            [jnp.where(upper, other, rows), jnp.where(upper, rows, other)], axis=0
        )
        bit = bit // 2
    return rows


def reduce_halves(values, devices):
    bit = 1
    while bit < devices:
        half = values.shape[0] // 2
        upper = my_bit(bit)
        low_part = values[:half]
        high_part = values[half:]
        keep = jnp.where(upper, high_part, low_part).astype(jnp.float32)
        sent = jnp.where(upper, low_part, high_part)
        values = (keep + exchange(sent, bit, devices).astype(jnp.float32)).astype(values.dtype)
        bit = bit * 2
    return values


def reverse_bits(count):
    width = count.bit_length() - 1
    return [int(format(i, "b").zfill(width)[::-1], 2) for i in range(count)]


def all_to_all(values):
    return lax.all_to_all(values, AXES, split_axis=0, concat_axis=0, tiled=True)


def pieces_of(rows, devices):
    return rows.reshape(-1, devices, BLOCK_ROWS * D // devices).transpose(1, 0, 2)


def rows_of(pieces):
    return pieces.transpose(1, 0, 2).reshape(-1, D)


def route_in(rows, small, place, slots, devices):
    pieces = pieces_of(rows, devices)
    piece = pieces.shape[2]
    extra = -(-small.shape[0] // piece)
    tail = jnp.pad(small, (0, extra * piece - small.shape[0])).reshape(1, extra, piece)
    tail = jnp.broadcast_to(tail, (devices, extra, piece))
    moved = all_to_all(jnp.concatenate([pieces, tail], axis=1))
    small_all = moved[:, -extra:].reshape(devices, -1)[:, : small.shape[0]].reshape(-1)
    pieces = moved[:, :-extra].reshape(slots, piece)
    chosen = place[:, None] == jnp.arange(slots, dtype=jnp.int32)[None, :]
    homed = product(chosen.astype(jnp.bfloat16), pieces).astype(jnp.bfloat16)
    return (rows_of(all_to_all(homed.reshape(devices, -1, piece))), small_all)


def route_out(rows, place, slots, devices):
    pieces = all_to_all(pieces_of(rows, devices)).reshape(place.shape[0], -1)
    chosen = place[:, None] == jnp.arange(slots, dtype=jnp.int32)[None, :]
    slotted = inner_rows(chosen.astype(jnp.bfloat16), pieces).astype(jnp.bfloat16)
    return rows_of(all_to_all(slotted.reshape(devices, -1, pieces.shape[1])))


KEY_BLOCKS = D // BLOCK_ROWS


def even_homes(blocks, devices):
    return KEY_BLOCKS % devices == 0 and (blocks - 2 * KEY_BLOCKS) % devices == 0


def home_order(slot, devices, turned_groups):
    order = jnp.array(reverse_bits(devices), dtype=jnp.int32)
    parts = []
    for group in range(turned_groups):
        part = slot[group * KEY_BLOCKS : (group + 1) * KEY_BLOCKS]
        parts.append(part.reshape(devices, -1)[order])
    parts.append(slot[turned_groups * KEY_BLOCKS :].reshape(devices, -1))
    return jnp.concatenate(parts, axis=1).reshape(-1)


def gather_rows(weights, small, slot, devices):
    slots = devices * (weights.shape[0] // BLOCK_ROWS)
    low = weights.astype(jnp.bfloat16)
    small = small.astype(jnp.bfloat16)
    if not even_homes(slot.shape[0], devices):
        rows = unpack_rows(lax.all_gather(low, AXES, axis=0, tiled=True), slot)
        return (rows, lax.all_gather(small, AXES, axis=0, tiled=True))
    homed, small_all = route_in(low, small, home_order(slot, devices, 1), slots, devices)
    share = D // devices
    rest = lax.all_gather(homed[share:], AXES, axis=0, tiled=True)
    keys = gather_doubling(homed[:share], devices)
    return ((keys, rest[:D], rest[D : D + FF], rest[D + FF :]), small_all)


def weight_grads_kernel(pre_ref, hidden_ref, active_ref, branch_ref, out_ref):
    step = pl.program_id(0)
    half = pl.num_programs(0) // 2

    @pl.when(step < half)
    def _():
        out_ref[...] = inner_rows(pre_ref[...], hidden_ref[...]).astype(jnp.bfloat16)

    @pl.when(step >= half)
    def _():
        out_ref[...] = inner_rows(active_ref[...], branch_ref[...]).astype(jnp.bfloat16)


def weight_grads(grad_pre, hidden_low, active, grad_branch):
    rows = grad_pre.shape[0]
    width = 512
    half = FF // width
    whole = pl.BlockSpec((rows, D), lambda i: (0, 0))
    return pl.pallas_call(
        weight_grads_kernel,
        out_shape=jax.ShapeDtypeStruct((2 * FF, D), jnp.bfloat16),
        grid=(2 * half,),
        in_specs=[
            pl.BlockSpec((rows, width), lambda i: (0, jnp.minimum(i, half - 1))),
            whole,
            pl.BlockSpec((rows, width), lambda i: (0, jnp.maximum(i - half, 0))),
            whole,
        ],
        out_specs=pl.BlockSpec((width, D), lambda i: (i, 0)),
        name="weight_grads",
    )(grad_pre, hidden_low, active, grad_branch)


def scatter_grads(grad_key, grad_out, grad_wide, small_grad, slot, slots, devices):
    blocks = slot.shape[0]
    if not even_homes(blocks, devices):
        rows = jnp.concatenate([grad_key, grad_out, grad_wide], axis=0)
        rows = rows.reshape(blocks, BLOCK_ROWS * D)
        chosen = slot[:, None] == jnp.arange(slots, dtype=jnp.int32)[None, :]
        slotted = inner_rows(chosen.astype(jnp.bfloat16), rows).astype(jnp.bfloat16)
        return (
            lax.psum_scatter(slotted.reshape(-1, D), AXES, scatter_dimension=0, tiled=True),
            lax.psum_scatter(small_grad, AXES, scatter_dimension=0, tiled=True),
        )
    wide_home = lax.psum_scatter(grad_wide, AXES, scatter_dimension=0, tiled=True)
    order = jnp.array(reverse_bits(devices), dtype=jnp.int32)
    share = D // devices
    small_share = small_grad.shape[0] // devices
    small_deep = -(-small_share // D)
    deep = -(-(2 * share + small_deep) // 8) * 8
    small_rows = small_grad.reshape(devices, small_share)[order].astype(jnp.bfloat16)
    small_rows = jnp.pad(
        small_rows, ((0, 0), (0, (deep - 2 * share) * D - small_share))
    ).reshape(devices, -1, D)
    packed = jnp.concatenate(
        [grad_key.reshape(devices, share, D), grad_out.reshape(devices, share, D), small_rows],
        axis=1,
    )
    summed = reduce_halves(packed.reshape(-1, D), devices)
    home = jnp.concatenate([summed[: 2 * share], wide_home], axis=0)
    small_home = summed[2 * share : 2 * share + small_deep].reshape(-1)[:small_share]
    return (
        route_out(home, home_order(slot, devices, 2), slots, devices).astype(jnp.float32),
        small_home.astype(jnp.float32),
    )


def adamw_update(master, first, second, grad, decay, rate):
    correct = 1.0 - 0.5**STEP
    first_new = 0.5 * first + 0.5 * grad
    second_new = 0.5 * second + 0.5 * grad * grad
    update = first_new / correct / (jnp.sqrt(second_new / correct) + 1e-08) + decay * master
    return (master - rate * update, first_new, second_new)


def body(
    hidden_in,
    cotangent,
    part_lengths,
    segment_start,
    query_weight,
    value_weight,
    shared_down,
    shared_up,
    owner,
    weights,
    first_moment,
    second_moment,
    small_weights,
    small_first,
    small_second,
):
    capacity = weights.shape[0] // BLOCK_ROWS
    devices = lax.axis_size("rows") * lax.axis_size("heads")
    slot = slot_index(owner, capacity)
    (key_rows, out_rows, up_rows, down_rows), small_all = gather_rows(
        weights, small_weights, slot, devices
    )
    (
        scale_q_rank,
        scale_v_rank,
        scale_q_out,
        scale_v_out,
        out_bias,
        up_bias,
        down_bias,
        gain_one,
        shift_one,
        gain_two,
        shift_two,
    ) = [piece.astype(jnp.float32) for piece in split_small(small_all)]
    projected = product(hidden_in, shared_down).astype(jnp.bfloat16)
    projected_wide = projected.astype(jnp.float32)
    rank_q = (scale_q_rank * projected_wide).astype(jnp.bfloat16)
    rank_v = (scale_v_rank * projected_wide).astype(jnp.bfloat16)
    side_q = product(rank_q, shared_up)
    side_v = product(rank_v, shared_up)
    query = (product(hidden_in, query_weight) + scale_q_out * side_q).astype(jnp.bfloat16)
    keys = product(hidden_in, key_rows).astype(jnp.bfloat16)
    values = (product(hidden_in, value_weight) + scale_v_out * side_v).astype(jnp.bfloat16)
    mine = lax.axis_index("heads")
    spans = jnp.concatenate([part_lengths[mine], segment_start[mine][None]])
    context, log_total = attend_forward(spans, query, keys, values)
    attended = product(context, out_rows) + out_bias
    first_sum = hidden_in.astype(jnp.float32) + attended
    norm_one, inverse_one = normalize(first_sum)
    hidden_one = norm_one * gain_one + shift_one
    hidden_low = hidden_one.astype(jnp.bfloat16)
    pre_act = product_t(hidden_low, up_rows) + up_bias
    share = 0.5 * (1.0 + lax.erf(pre_act * 0.7071067811865476))
    slope = share + pre_act * jnp.exp(-0.5 * pre_act * pre_act) * 0.3989422804014327
    active, slope = lax.optimization_barrier(
        ((pre_act * share).astype(jnp.bfloat16), slope.astype(jnp.bfloat16))
    )
    second_sum = hidden_one + product(active, down_rows) + down_bias
    norm_two, inverse_two = normalize(second_sum)
    block_out = (norm_two * gain_two + shift_two).astype(jnp.bfloat16)
    grad_top = cotangent.astype(jnp.float32)
    grad_gain_two = jnp.sum(grad_top * norm_two, axis=0)
    grad_shift_two = jnp.sum(grad_top, axis=0)
    grad_second = norm_back(grad_top * gain_two, norm_two, inverse_two)
    grad_branch = grad_second.astype(jnp.bfloat16)
    grad_down_bias = jnp.sum(grad_branch.astype(jnp.float32), axis=0)
    grad_pre = (product_t(grad_branch, down_rows) * slope.astype(jnp.float32)).astype(jnp.bfloat16)
    grad_up_bias = jnp.sum(grad_pre.astype(jnp.float32), axis=0)
    grad_wide = weight_grads(grad_pre, hidden_low, active, grad_branch)
    grad_hidden = grad_second + product(grad_pre, up_rows)
    grad_gain_one = jnp.sum(grad_hidden * norm_one, axis=0)
    grad_shift_one = jnp.sum(grad_hidden, axis=0)
    grad_first = norm_back(grad_hidden * gain_one, norm_one, inverse_one)
    grad_attended = grad_first.astype(jnp.bfloat16)
    grad_out_bias = jnp.sum(grad_attended.astype(jnp.float32), axis=0)
    grad_out = inner_rows(context, grad_attended).astype(jnp.bfloat16)
    grad_context = product_t(grad_attended, out_rows).astype(jnp.bfloat16)
    grad_query, grad_keys, grad_values = attend_backward(
        spans, query, keys, values, context, grad_context, log_total
    )
    grad_key = inner_rows(hidden_in, grad_keys).astype(jnp.bfloat16)
    grad_query_wide = grad_query.astype(jnp.float32)
    grad_values_wide = grad_values.astype(jnp.float32)
    grad_scale_q_out = jnp.sum(grad_query_wide * side_q, axis=0)
    grad_scale_v_out = jnp.sum(grad_values_wide * side_v, axis=0)
    grad_side_q = (scale_q_out * grad_query_wide).astype(jnp.bfloat16)
    grad_side_v = (scale_v_out * grad_values_wide).astype(jnp.bfloat16)
    grad_rank_q = product_t(grad_side_q, shared_up)
    grad_rank_v = product_t(grad_side_v, shared_up)
    grad_scale_q_rank = jnp.sum(grad_rank_q * projected_wide, axis=0)
    grad_scale_v_rank = jnp.sum(grad_rank_v * projected_wide, axis=0)
    grad_projected = (grad_rank_q * scale_q_rank + grad_rank_v * scale_v_rank).astype(jnp.bfloat16)
    grad_input = grad_first + product_t(grad_query, query_weight) + product_t(grad_keys, key_rows)
    grad_input = (
        grad_input + product_t(grad_values, value_weight) + product_t(grad_projected, shared_down)
    )
    input_grad = grad_input.astype(jnp.bfloat16)
    small_grad = jnp.concatenate(
        [
            grad_scale_q_rank,
            grad_scale_v_rank,
            grad_scale_q_out,
            grad_scale_v_out,
            grad_out_bias,
            grad_up_bias,
            grad_down_bias,
            grad_gain_one,
            grad_shift_one,
            grad_gain_two,
            grad_shift_two,
        ]
    )
    owned_grad, owned_small = scatter_grads(
        grad_key, grad_out, grad_wide, small_grad, slot, devices * capacity, devices
    )
    new_weights, new_first, new_second = adamw_update(
        weights, first_moment, second_moment, owned_grad, 0.01, 0.03
    )
    new_small, new_small_first, new_small_second = adamw_update(
        small_weights, small_first, small_second, owned_small, 0.0, 0.3
    )
    return (
        block_out,
        input_grad,
        new_weights,
        new_first,
        new_second,
        new_weights.astype(jnp.bfloat16),
        new_small,
        new_small_first,
        new_small_second,
        new_small.astype(jnp.bfloat16),
    )


def solution(mesh):
    return jax.shard_map(
        body,
        mesh=mesh,
        in_specs=(
            P(("rows", "heads"), None),
            P(("rows", "heads"), None),
            P("rows", None),
            P("rows"),
            P(),
            P(),
            P(),
            P(),
            P(),
            P(("rows", "heads"), None),
            P(("rows", "heads"), None),
            P(("rows", "heads"), None),
            P(("rows", "heads")),
            P(("rows", "heads")),
            P(("rows", "heads")),
        ),
        out_specs=(
            P(("rows", "heads"), None),
            P(("rows", "heads"), None),
            P(("rows", "heads"), None),
            P(("rows", "heads"), None),
            P(("rows", "heads"), None),
            P(("rows", "heads"), None),
            P(("rows", "heads")),
            P(("rows", "heads")),
            P(("rows", "heads")),
            P(("rows", "heads")),
        ),
        check_vma=False,
    )
```

```python
import jax
import jax.numpy as jnp
from jax import lax
from jax.experimental import pallas as pl
from jax.experimental.pallas import tpu as pltpu
from jax.sharding import PartitionSpec as P

D = 768
FF = 3072
HEAD_DIM = 64
RANK = 1024
SEQ_LEN = 1024
STEP = 3
BLOCK_ROWS = 12


def slot_index(owner, capacity):
    count = owner.shape[0]
    order = jnp.arange(count, dtype=jnp.int32)
    same_owner = owner[:, None] == owner[None, :]
    earlier = order[None, :] < order[:, None]
    ranked = jnp.sum((same_owner & earlier).astype(jnp.int32), axis=1)
    return owner * capacity + ranked


def split_small(vector):
    widths = [RANK, RANK, D, D, D, FF, D, D, D, D, D]
    pieces = []
    offset = 0
    for width in widths:
        pieces.append(vector[offset : offset + width])
        offset = offset + width
    return pieces


def unpack_rows(gathered, slot):
    rows = gathered.reshape(-1, BLOCK_ROWS, D)[slot].reshape(-1, D)
    return (rows[:D], rows[D : 2 * D], rows[2 * D : 2 * D + FF], rows[2 * D + FF :])


def product(left, right):
    return jnp.dot(left, right, preferred_element_type=jnp.float32)


def product_t(left, right):
    return lax.dot_general(
        left, right, (((1,), (1,)), ((), ())), preferred_element_type=jnp.float32
    )


def inner_rows(left, right):
    return lax.dot_general(
        left, right, (((0,), (0,)), ((), ())), preferred_element_type=jnp.float32
    )


def normalize(values):
    centre = jnp.mean(values, axis=-1, keepdims=True)
    centred = values - centre
    spread = jnp.mean(centred * centred, axis=-1, keepdims=True)
    inverse = lax.rsqrt(spread + 1e-05)
    return (centred * inverse, inverse)


def norm_back(grad_norm, normed, inverse):
    first_mean = jnp.mean(grad_norm, axis=-1, keepdims=True)
    second_mean = jnp.mean(grad_norm * normed, axis=-1, keepdims=True)
    return inverse * (grad_norm - first_mean - normed * second_mean)


PAIR = 2 * HEAD_DIM
TILE = 256


def lane_split(rows):
    return lax.broadcasted_iota(jnp.int32, (rows, PAIR), 1)


def visible_bias(spans, rows):
    place = lax.broadcasted_iota(jnp.int32, (rows, PAIR), 0)
    first_end = spans[0]
    begin = spans[2]
    seen = (place < first_end) | ((place >= begin) & (place < begin + spans[1]))
    return jnp.where(seen, 0.0, -1e30)


def score_operands(query, keys, bias, lanes, half):
    mine = (lanes < HEAD_DIM) == (half == 0)
    spare = lanes == (HEAD_DIM if half == 0 else 0)
    query_h = jnp.where(mine, query * 0.125, jnp.where(spare, 1.0, 0.0)).astype(jnp.bfloat16)
    keys_h = jnp.where(mine, keys, bias).astype(jnp.bfloat16)
    return (mine, query_h, keys_h)


def attend_forward_kernel(spans, query_ref, keys_ref, values_ref, context_ref, total_ref, turned):
    rows = query_ref.shape[0]
    lanes = lane_split(rows)
    bias = visible_bias(spans, rows)
    query = query_ref[...].astype(jnp.float32)
    keys = keys_ref[...].astype(jnp.float32)
    values_t = values_ref[...].astype(jnp.float32).T
    feature = lax.broadcasted_iota(jnp.int32, values_t.shape, 0)
    operands = []
    for half in range(2):
        _, query_h, keys_h = score_operands(query, keys, bias, lanes, half)
        own = (feature < HEAD_DIM) == (half == 0)
        operands.append((query_h, keys_h, jnp.where(own, values_t, 1.0).astype(jnp.bfloat16)))
    steps = [(half, start) for half in range(2) for start in range(0, rows, TILE)]

    def scores_of(step):
        half, start = step
        return product_t(operands[half][1], operands[half][0][start : start + TILE])

    ready = [scores_of(step) for step in steps[:2]]
    for index, (half, start) in enumerate(steps):
        if index + 2 < len(steps):
            ready.append(scores_of(steps[index + 2]))
        scores = ready.pop(0)
        low = half * HEAD_DIM
        other = HEAD_DIM - low
        highest = jnp.max(scores, axis=0, keepdims=True)
        raised = jnp.exp(scores - highest).astype(jnp.bfloat16)
        mixed = product(operands[half][2], raised)
        summed = mixed[other : other + 1]
        total_ref[0, half : half + 1, start : start + TILE] = highest + jnp.log(summed)
        turned[low : low + HEAD_DIM, start : start + TILE] = mixed[low : low + HEAD_DIM] / summed
    context_ref[...] = turned[...].T.astype(jnp.bfloat16)


def attend_backward_kernel(
    spans,
    query_ref,
    keys_ref,
    values_ref,
    context_ref,
    grad_ref,
    total_ref,
    grad_query_ref,
    grad_keys_ref,
    grad_values_ref,
    turned,
    keys_sum,
    values_sum,
):
    rows = query_ref.shape[0]
    lanes = lane_split(rows)
    bias = visible_bias(spans, rows)
    query = query_ref[...].astype(jnp.float32)
    keys = keys_ref[...].astype(jnp.float32)
    values = values_ref[...].astype(jnp.float32)
    grad = grad_ref[...].astype(jnp.float32)
    dots = (grad * context_ref[...].astype(jnp.float32)).T
    keys_t = keys.T
    feature = lax.broadcasted_iota(jnp.int32, keys_t.shape, 0)
    grad_low = grad_ref[...]
    for half in range(2):
        mine, query_h, keys_h = score_operands(query, keys, bias, lanes, half)
        values_h = jnp.where(mine, values, 0.0).astype(jnp.bfloat16)
        grad_h = jnp.where(mine, grad, 0.0).astype(jnp.bfloat16)
        query_m = jnp.where(mine, query * 0.125, 0.0).astype(jnp.bfloat16)
        own = (feature < HEAD_DIM) == (half == 0)
        keys_th = jnp.where(own, keys_t * 0.125, 0.0).astype(jnp.bfloat16)
        low = half * HEAD_DIM
        row_dot = jnp.sum(dots[low : low + HEAD_DIM], axis=0, keepdims=True)
        for start in range(0, rows, TILE):
            part = slice(start, start + TILE)
            scores = product_t(keys_h, query_h[part])
            probs = jnp.exp(scores - total_ref[0, half : half + 1, part])
            grad_probs = product_t(values_h, grad_low[part])
            grad_scores = (probs * (grad_probs - row_dot[:, part])).astype(jnp.bfloat16)
            values_part = product(probs.astype(jnp.bfloat16), grad_h[part])
            keys_part = product(grad_scores, query_m[part])
            query_part = product(keys_th, grad_scores)
            if half == 0 and start == 0:
                values_sum[...] = values_part
                keys_sum[...] = keys_part
            else:
                values_sum[...] += values_part
                keys_sum[...] += keys_part
            if half == 0:
                turned[:, part] = query_part
            else:
                turned[:, part] += query_part
    grad_query_ref[...] = turned[...].T.astype(jnp.bfloat16)
    grad_keys_ref[...] = keys_sum[...].astype(jnp.bfloat16)
    grad_values_ref[...] = values_sum[...].astype(jnp.bfloat16)


def pair_specs(rows):
    wide = pl.BlockSpec((rows, PAIR), lambda i, spans: (0, i))
    total = pl.BlockSpec((1, 2, rows), lambda i, spans: (i, 0, 0))
    return (wide, total)


def attend_forward(spans, query, keys, values):
    rows, width = query.shape
    pairs = width // PAIR
    wide, total = pair_specs(rows)
    return pl.pallas_call(
        attend_forward_kernel,
        out_shape=(
            jax.ShapeDtypeStruct((rows, width), jnp.bfloat16),
            jax.ShapeDtypeStruct((pairs, 2, rows), jnp.float32),
        ),
        grid_spec=pltpu.PrefetchScalarGridSpec(
            num_scalar_prefetch=1,
            grid=(pairs,),
            in_specs=[wide, wide, wide],
            out_specs=(wide, total),
            scratch_shapes=[pltpu.VMEM((PAIR, rows), jnp.float32)],
        ),
        name="attend_forward",
    )(spans, query, keys, values)


def attend_backward(spans, query, keys, values, context, grad_context, log_total):
    rows, width = query.shape
    pairs = width // PAIR
    wide, total = pair_specs(rows)
    shape = jax.ShapeDtypeStruct((rows, width), jnp.bfloat16)
    return pl.pallas_call(
        attend_backward_kernel,
        out_shape=(shape, shape, shape),
        grid_spec=pltpu.PrefetchScalarGridSpec(
            num_scalar_prefetch=1,
            grid=(pairs,),
            in_specs=[wide, wide, wide, wide, wide, total],
            out_specs=(wide, wide, wide),
            scratch_shapes=[
                pltpu.VMEM((PAIR, rows), jnp.float32),
                pltpu.VMEM((rows, PAIR), jnp.float32),
                pltpu.VMEM((rows, PAIR), jnp.float32),
            ],
        ),
        name="attend_backward",
    )(spans, query, keys, values, context, grad_context, log_total)


AXES = ("rows", "heads")


def exchange(values, bit, devices):
    return lax.ppermute(values, AXES, [(i, i ^ bit) for i in range(devices)])


def my_bit(bit):
    return (lax.axis_index(AXES) & bit) != 0


def gather_doubling(rows, devices):
    share = rows.shape[0]
    rows = rows[None]
    bit = devices // 2
    while bit:
        other = exchange(rows, bit, devices)
        upper = my_bit(bit)
        rows = jnp.concatenate(
            [jnp.where(upper, other, rows), jnp.where(upper, rows, other)], axis=1
        ).reshape(-1, share, D)
        bit = bit // 2
    return rows.reshape(-1, D)


def reduce_halves(values, devices):
    bit = 1
    while bit < devices:
        values = values.reshape(values.shape[0] // 2, 2, *values.shape[1:])
        upper = my_bit(bit)
        keep = jnp.where(upper, values[:, 1], values[:, 0]).astype(jnp.float32)
        sent = jnp.where(upper, values[:, 0], values[:, 1])
        values = (keep + exchange(sent, bit, devices).astype(jnp.float32)).astype(values.dtype)
        bit = bit * 2
    return values[0]


def all_to_all(values):
    return lax.all_to_all(values, AXES, split_axis=0, concat_axis=0, tiled=True)


def pieces_of(rows, devices):
    return rows.reshape(-1, devices, BLOCK_ROWS * D // devices).transpose(1, 0, 2)


def rows_of(pieces):
    return pieces.transpose(1, 0, 2).reshape(-1, D)


def route_in(rows, small, place, slots, devices):
    pieces = pieces_of(rows, devices)
    piece = pieces.shape[2]
    extra = -(-small.shape[0] // piece)
    tail = jnp.pad(small, (0, extra * piece - small.shape[0])).reshape(1, extra, piece)
    tail = jnp.broadcast_to(tail, (devices, extra, piece))
    moved = all_to_all(jnp.concatenate([pieces, tail], axis=1))
    small_all = moved[:, -extra:].reshape(devices, -1)[:, : small.shape[0]].reshape(-1)
    pieces = moved[:, :-extra].reshape(slots, piece)
    chosen = place[:, None] == jnp.arange(slots, dtype=jnp.int32)[None, :]
    homed = product(chosen.astype(jnp.bfloat16), pieces).astype(jnp.bfloat16)
    return (rows_of(all_to_all(homed.reshape(devices, -1, piece))), small_all)


def assemble_kernel(pieces_ref, out_ref, lines, columns):
    devices, slots, _ = pieces_ref.shape
    wide = D // devices
    for row in range(BLOCK_ROWS):
        for piece in range(devices):
            lines[row * slots : (row + 1) * slots, piece * wide : (piece + 1) * wide] = pieces_ref[
                piece, :, row * wide : (row + 1) * wide
            ].astype(jnp.float32)
    for group in range(D // PAIR):
        lanes = slice(group * PAIR, (group + 1) * PAIR)
        for row in range(BLOCK_ROWS):
            columns[group, pl.ds(row, slots, stride=BLOCK_ROWS), :] = lines[
                row * slots : (row + 1) * slots, lanes
            ]
        out_ref[:, lanes] = columns[group]


def assemble(pieces):
    rows = pieces.shape[1] * BLOCK_ROWS
    return pl.pallas_call(
        assemble_kernel,
        out_shape=jax.ShapeDtypeStruct((rows, D), jnp.float32),
        scratch_shapes=[
            pltpu.VMEM((rows, D), jnp.float32),
            pltpu.VMEM((D // PAIR, rows, PAIR), jnp.float32),
        ],
        name="assemble",
    )(pieces)


def route_out(columns, slot, slots, devices):
    pieces = columns.T.reshape(slot.shape[0], -1)
    chosen = slot[:, None] == jnp.arange(slots, dtype=jnp.int32)[None, :]
    slotted = inner_rows(chosen.astype(jnp.bfloat16), pieces).astype(jnp.bfloat16)
    return assemble(all_to_all(slotted.reshape(devices, -1, pieces.shape[1])))


KEY_BLOCKS = D // BLOCK_ROWS


def even_homes(blocks, devices):
    return KEY_BLOCKS % devices == 0 and (blocks - 2 * KEY_BLOCKS) % devices == 0


def gather_rows(weights, small, slot, devices):
    slots = devices * (weights.shape[0] // BLOCK_ROWS)
    low = weights.astype(jnp.bfloat16)
    small = small.astype(jnp.bfloat16)
    if not even_homes(slot.shape[0], devices):
        rows = unpack_rows(lax.all_gather(low, AXES, axis=0, tiled=True), slot)
        return (rows, lax.all_gather(small, AXES, axis=0, tiled=True))
    place = jnp.concatenate(
        [slot[KEY_BLOCKS:].reshape(devices, -1), slot[:KEY_BLOCKS].reshape(devices, -1)], axis=1
    ).reshape(-1)
    homed, small_all = route_in(low, small, place, slots, devices)
    split = homed.shape[0] - D // devices
    rest = lax.all_gather(homed[:split], AXES, axis=0, tiled=True)
    keys = gather_doubling(homed[split:], devices)
    return ((keys, rest[:D], rest[D : D + FF], rest[D + FF :]), small_all)


def weight_grads_kernel(pre_ref, hidden_ref, active_ref, branch_ref, out_ref, turned):
    step = pl.program_id(0)
    half = pl.num_programs(0) // 2

    @pl.when(step == 0)
    def _():
        turned[...] = hidden_ref[...].T

    @pl.when(step == half)
    def _():
        turned[...] = branch_ref[...].T

    @pl.when(step < half)
    def _():
        out_ref[...] = product(turned[...], pre_ref[...]).astype(jnp.bfloat16)

    @pl.when(step >= half)
    def _():
        out_ref[...] = product(turned[...], active_ref[...]).astype(jnp.bfloat16)


def weight_grads(grad_pre, hidden_low, active, grad_branch):
    rows = grad_pre.shape[0]
    width = 1024
    half = FF // width
    whole = pl.BlockSpec((rows, D), lambda i: (0, 0))
    return pl.pallas_call(
        weight_grads_kernel,
        out_shape=jax.ShapeDtypeStruct((D, 2 * FF), jnp.bfloat16),
        grid=(2 * half,),
        in_specs=[
            pl.BlockSpec((rows, width), lambda i: (0, jnp.minimum(i, half - 1))),
            whole,
            pl.BlockSpec((rows, width), lambda i: (0, jnp.maximum(i - half, 0))),
            whole,
        ],
        out_specs=pl.BlockSpec((D, width), lambda i: (0, i)),
        scratch_shapes=[pltpu.VMEM((D, rows), jnp.bfloat16)],
        name="weight_grads",
    )(grad_pre, hidden_low, active, grad_branch)


def scatter_grads(grad_key, grad_out, grad_wide, small_grad, slot, slots, devices):
    blocks = slot.shape[0]
    if not even_homes(blocks, devices):
        rows = jnp.concatenate([grad_key, grad_out, grad_wide], axis=1).T
        rows = rows.reshape(blocks, BLOCK_ROWS * D)
        chosen = slot[:, None] == jnp.arange(slots, dtype=jnp.int32)[None, :]
        slotted = inner_rows(chosen.astype(jnp.bfloat16), rows).astype(jnp.bfloat16)
        return (
            lax.psum_scatter(slotted.reshape(-1, D), AXES, scatter_dimension=0, tiled=True),
            lax.psum_scatter(small_grad, AXES, scatter_dimension=0, tiled=True),
        )
    wide_part = lax.psum_scatter(grad_wide, AXES, scatter_dimension=0, tiled=True)
    share = D // devices
    small_share = small_grad.shape[0] // devices
    small_deep = -(-small_share // D)
    deep = -(-(2 * share + small_deep) // 8) * 8 - 2 * share
    small_rows = jnp.pad(
        small_grad.reshape(devices, small_share).astype(jnp.bfloat16),
        ((0, 0), (0, deep * D - small_share)),
    ).reshape(devices, deep, D)
    packed = jnp.concatenate(
        [grad_key.reshape(devices, share, D), grad_out.reshape(devices, share, D), small_rows],
        axis=1,
    )
    summed = reduce_halves(packed, devices)
    columns = jnp.concatenate([summed[:share], summed[share : 2 * share], wide_part], axis=1)
    small_part = summed[2 * share : 2 * share + small_deep].reshape(-1)[:small_share]
    return (route_out(columns, slot, slots, devices), small_part.astype(jnp.float32))


def adamw_update(master, first, second, grad, decay, rate):
    correct = 1.0 - 0.5**STEP
    first_new = 0.5 * first + 0.5 * grad
    second_new = 0.5 * second + 0.5 * grad * grad
    update = first_new / correct / (jnp.sqrt(second_new / correct) + 1e-08) + decay * master
    return (master - rate * update, first_new, second_new)


def body(
    hidden_in,
    cotangent,
    part_lengths,
    segment_start,
    query_weight,
    value_weight,
    shared_down,
    shared_up,
    owner,
    weights,
    first_moment,
    second_moment,
    small_weights,
    small_first,
    small_second,
):
    capacity = weights.shape[0] // BLOCK_ROWS
    devices = lax.axis_size("rows") * lax.axis_size("heads")
    slot = slot_index(owner, capacity)
    (key_rows, out_rows, up_rows, down_rows), small_all = gather_rows(
        weights, small_weights, slot, devices
    )
    (
        scale_q_rank,
        scale_v_rank,
        scale_q_out,
        scale_v_out,
        out_bias,
        up_bias,
        down_bias,
        gain_one,
        shift_one,
        gain_two,
        shift_two,
    ) = [piece.astype(jnp.float32) for piece in split_small(small_all)]
    projected = product(hidden_in, shared_down).astype(jnp.bfloat16)
    projected_wide = projected.astype(jnp.float32)
    rank_q = (scale_q_rank * projected_wide).astype(jnp.bfloat16)
    rank_v = (scale_v_rank * projected_wide).astype(jnp.bfloat16)
    side_q = product(rank_q, shared_up)
    side_v = product(rank_v, shared_up)
    query = (product(hidden_in, query_weight) + scale_q_out * side_q).astype(jnp.bfloat16)
    keys = product(hidden_in, key_rows).astype(jnp.bfloat16)
    values = (product(hidden_in, value_weight) + scale_v_out * side_v).astype(jnp.bfloat16)
    mine = lax.axis_index("heads")
    spans = jnp.concatenate([part_lengths[mine], segment_start[mine][None]])
    context, log_total = attend_forward(spans, query, keys, values)
    attended = product(context, out_rows) + out_bias
    first_sum = hidden_in.astype(jnp.float32) + attended
    norm_one, inverse_one = normalize(first_sum)
    hidden_one = norm_one * gain_one + shift_one
    hidden_low = hidden_one.astype(jnp.bfloat16)
    pre_act = product_t(hidden_low, up_rows) + up_bias
    share = 0.5 * (1.0 + lax.erf(pre_act * 0.7071067811865476))
    slope = share + pre_act * jnp.exp(-0.5 * pre_act * pre_act) * 0.3989422804014327
    active, slope = lax.optimization_barrier(
        ((pre_act * share).astype(jnp.bfloat16), slope.astype(jnp.bfloat16))
    )
    second_sum = hidden_one + product(active, down_rows) + down_bias
    norm_two, inverse_two = normalize(second_sum)
    block_out = (norm_two * gain_two + shift_two).astype(jnp.bfloat16)
    grad_top = cotangent.astype(jnp.float32)
    grad_gain_two = jnp.sum(grad_top * norm_two, axis=0)
    grad_shift_two = jnp.sum(grad_top, axis=0)
    grad_second = norm_back(grad_top * gain_two, norm_two, inverse_two)
    grad_branch = grad_second.astype(jnp.bfloat16)
    grad_down_bias = jnp.sum(grad_branch.astype(jnp.float32), axis=0)
    grad_pre = (product_t(grad_branch, down_rows) * slope.astype(jnp.float32)).astype(jnp.bfloat16)
    grad_up_bias = jnp.sum(grad_pre.astype(jnp.float32), axis=0)
    grad_wide = weight_grads(grad_pre, hidden_low, active, grad_branch)
    grad_hidden = grad_second + product(grad_pre, up_rows)
    grad_gain_one = jnp.sum(grad_hidden * norm_one, axis=0)
    grad_shift_one = jnp.sum(grad_hidden, axis=0)
    grad_first = norm_back(grad_hidden * gain_one, norm_one, inverse_one)
    grad_attended = grad_first.astype(jnp.bfloat16)
    grad_out_bias = jnp.sum(grad_attended.astype(jnp.float32), axis=0)
    grad_out = inner_rows(grad_attended, context).astype(jnp.bfloat16)
    grad_context = product_t(grad_attended, out_rows).astype(jnp.bfloat16)
    grad_query, grad_keys, grad_values = attend_backward(
        spans, query, keys, values, context, grad_context, log_total
    )
    grad_key = inner_rows(grad_keys, hidden_in).astype(jnp.bfloat16)
    grad_query_wide = grad_query.astype(jnp.float32)
    grad_values_wide = grad_values.astype(jnp.float32)
    grad_scale_q_out = jnp.sum(grad_query_wide * side_q, axis=0)
    grad_scale_v_out = jnp.sum(grad_values_wide * side_v, axis=0)
    grad_side_q = (scale_q_out * grad_query_wide).astype(jnp.bfloat16)
    grad_side_v = (scale_v_out * grad_values_wide).astype(jnp.bfloat16)
    grad_rank_q = product_t(grad_side_q, shared_up)
    grad_rank_v = product_t(grad_side_v, shared_up)
    grad_scale_q_rank = jnp.sum(grad_rank_q * projected_wide, axis=0)
    grad_scale_v_rank = jnp.sum(grad_rank_v * projected_wide, axis=0)
    grad_projected = (grad_rank_q * scale_q_rank + grad_rank_v * scale_v_rank).astype(jnp.bfloat16)
    grad_input = grad_first + product_t(grad_query, query_weight) + product_t(grad_keys, key_rows)
    grad_input = (
        grad_input + product_t(grad_values, value_weight) + product_t(grad_projected, shared_down)
    )
    input_grad = grad_input.astype(jnp.bfloat16)
    small_grad = jnp.concatenate(
        [
            grad_scale_q_rank,
            grad_scale_v_rank,
            grad_scale_q_out,
            grad_scale_v_out,
            grad_out_bias,
            grad_up_bias,
            grad_down_bias,
            grad_gain_one,
            grad_shift_one,
            grad_gain_two,
            grad_shift_two,
        ]
    )
    owned_grad, owned_small = scatter_grads(
        grad_key, grad_out, grad_wide, small_grad, slot, devices * capacity, devices
    )
    new_weights, new_first, new_second = adamw_update(
        weights, first_moment, second_moment, owned_grad, 0.01, 0.03
    )
    new_small, new_small_first, new_small_second = adamw_update(
        small_weights, small_first, small_second, owned_small, 0.0, 0.3
    )
    return (
        block_out,
        input_grad,
        new_weights,
        new_first,
        new_second,
        new_weights.astype(jnp.bfloat16),
        new_small,
        new_small_first,
        new_small_second,
        new_small.astype(jnp.bfloat16),
    )


def solution(mesh):
    return jax.shard_map(
        body,
        mesh=mesh,
        in_specs=(
            P(("rows", "heads"), None),
            P(("rows", "heads"), None),
            P("rows", None),
            P("rows"),
            P(),
            P(),
            P(),
            P(),
            P(),
            P(("rows", "heads"), None),
            P(("rows", "heads"), None),
            P(("rows", "heads"), None),
            P(("rows", "heads")),
            P(("rows", "heads")),
            P(("rows", "heads")),
        ),
        out_specs=(
            P(("rows", "heads"), None),
            P(("rows", "heads"), None),
            P(("rows", "heads"), None),
            P(("rows", "heads"), None),
            P(("rows", "heads"), None),
            P(("rows", "heads"), None),
            P(("rows", "heads")),
            P(("rows", "heads")),
            P(("rows", "heads")),
            P(("rows", "heads")),
        ),
        check_vma=False,
    )
```

```python
import jax
import jax.numpy as jnp
from jax import lax
from jax.experimental import pallas as pl
from jax.experimental.pallas import tpu as pltpu
from jax.sharding import PartitionSpec as P

D = 768
FF = 3072
HEAD_DIM = 64
RANK = 1024
SEQ_LEN = 1024
STEP = 3
BLOCK_ROWS = 12


def slot_index(owner, capacity):
    count = owner.shape[0]
    order = jnp.arange(count, dtype=jnp.int32)
    same_owner = owner[:, None] == owner[None, :]
    earlier = order[None, :] < order[:, None]
    ranked = jnp.sum((same_owner & earlier).astype(jnp.int32), axis=1)
    return owner * capacity + ranked


def split_small(vector):
    widths = [RANK, RANK, D, D, D, FF, D, D, D, D, D]
    pieces = []
    offset = 0
    for width in widths:
        pieces.append(vector[offset : offset + width])
        offset = offset + width
    return pieces


def unpack_rows(gathered, slot):
    rows = gathered.reshape(-1, BLOCK_ROWS, D)[slot].reshape(-1, D)
    return (rows[:D], rows[D : 2 * D], rows[2 * D : 2 * D + FF], rows[2 * D + FF :])


def product(left, right):
    return jnp.dot(left, right, preferred_element_type=jnp.float32)


def product_t(left, right):
    return lax.dot_general(
        left, right, (((1,), (1,)), ((), ())), preferred_element_type=jnp.float32
    )


def inner_rows(left, right):
    return lax.dot_general(
        left, right, (((0,), (0,)), ((), ())), preferred_element_type=jnp.float32
    )


def normalize(values):
    centre = jnp.mean(values, axis=-1, keepdims=True)
    centred = values - centre
    spread = jnp.mean(centred * centred, axis=-1, keepdims=True)
    inverse = lax.rsqrt(spread + 1e-05)
    return (centred * inverse, inverse)


def norm_back(grad_norm, normed, inverse):
    first_mean = jnp.mean(grad_norm, axis=-1, keepdims=True)
    second_mean = jnp.mean(grad_norm * normed, axis=-1, keepdims=True)
    return inverse * (grad_norm - first_mean - normed * second_mean)


PAIR = 2 * HEAD_DIM
TILE = 256


def lane_split(rows):
    return lax.broadcasted_iota(jnp.int32, (rows, PAIR), 1)


def visible_bias(spans, rows):
    place = lax.broadcasted_iota(jnp.int32, (rows, PAIR), 0)
    first_end = spans[0]
    begin = spans[2]
    seen = (place < first_end) | ((place >= begin) & (place < begin + spans[1]))
    return jnp.where(seen, 0.0, -1e30)


def score_operands(query, keys, bias, lanes, half):
    mine = (lanes < HEAD_DIM) == (half == 0)
    spare = lanes == (HEAD_DIM if half == 0 else 0)
    query_h = jnp.where(mine, query * 0.125, jnp.where(spare, 1.0, 0.0)).astype(jnp.bfloat16)
    keys_h = jnp.where(mine, keys, bias).astype(jnp.bfloat16)
    return (mine, query_h, keys_h)


def attend_forward_kernel(spans, query_ref, keys_ref, values_ref, context_ref, total_ref, turned):
    rows = query_ref.shape[0]
    lanes = lane_split(rows)
    bias = visible_bias(spans, rows)
    query = query_ref[...].astype(jnp.float32)
    keys = keys_ref[...].astype(jnp.float32)
    values_t = values_ref[...].astype(jnp.float32).T
    feature = lax.broadcasted_iota(jnp.int32, values_t.shape, 0)
    operands = []
    for half in range(2):
        _, query_h, keys_h = score_operands(query, keys, bias, lanes, half)
        own = (feature < HEAD_DIM) == (half == 0)
        operands.append((query_h, keys_h, jnp.where(own, values_t, 1.0).astype(jnp.bfloat16)))
    steps = [(half, start) for half in range(2) for start in range(0, rows, TILE)]

    def scores_of(step):
        half, start = step
        return product_t(operands[half][1], operands[half][0][start : start + TILE])

    ready = [scores_of(step) for step in steps[:2]]
    for index, (half, start) in enumerate(steps):
        if index + 2 < len(steps):
            ready.append(scores_of(steps[index + 2]))
        scores = ready.pop(0)
        low = half * HEAD_DIM
        other = HEAD_DIM - low
        highest = jnp.max(scores, axis=0, keepdims=True)
        raised = jnp.exp(scores - highest).astype(jnp.bfloat16)
        mixed = product(operands[half][2], raised)
        summed = mixed[other : other + 1]
        total_ref[0, half : half + 1, start : start + TILE] = highest + jnp.log(summed)
        turned[low : low + HEAD_DIM, start : start + TILE] = mixed[low : low + HEAD_DIM] / summed
    context_ref[...] = turned[...].T.astype(jnp.bfloat16)


def attend_backward_kernel(
    spans,
    query_ref,
    keys_ref,
    values_ref,
    context_ref,
    grad_ref,
    total_ref,
    grad_query_ref,
    grad_keys_ref,
    grad_values_ref,
    turned,
    keys_sum,
    values_sum,
):
    rows = query_ref.shape[0]
    lanes = lane_split(rows)
    bias = visible_bias(spans, rows)
    query = query_ref[...].astype(jnp.float32)
    keys = keys_ref[...].astype(jnp.float32)
    values = values_ref[...].astype(jnp.float32)
    grad = grad_ref[...].astype(jnp.float32)
    dots = (grad * context_ref[...].astype(jnp.float32)).T
    keys_t = keys.T
    feature = lax.broadcasted_iota(jnp.int32, keys_t.shape, 0)
    grad_low = grad_ref[...]
    for half in range(2):
        mine, query_h, keys_h = score_operands(query, keys, bias, lanes, half)
        values_h = jnp.where(mine, values, 0.0).astype(jnp.bfloat16)
        grad_h = jnp.where(mine, grad, 0.0).astype(jnp.bfloat16)
        query_m = jnp.where(mine, query * 0.125, 0.0).astype(jnp.bfloat16)
        own = (feature < HEAD_DIM) == (half == 0)
        keys_th = jnp.where(own, keys_t * 0.125, 0.0).astype(jnp.bfloat16)
        low = half * HEAD_DIM
        row_dot = jnp.sum(dots[low : low + HEAD_DIM], axis=0, keepdims=True)
        for start in range(0, rows, TILE):
            part = slice(start, start + TILE)
            scores = product_t(keys_h, query_h[part])
            probs = jnp.exp(scores - total_ref[0, half : half + 1, part])
            grad_probs = product_t(values_h, grad_low[part])
            grad_scores = (probs * (grad_probs - row_dot[:, part])).astype(jnp.bfloat16)
            values_part = product(probs.astype(jnp.bfloat16), grad_h[part])
            keys_part = product(grad_scores, query_m[part])
            query_part = product(keys_th, grad_scores)
            if half == 0 and start == 0:
                values_sum[...] = values_part
                keys_sum[...] = keys_part
            else:
                values_sum[...] += values_part
                keys_sum[...] += keys_part
            if half == 0:
                turned[:, part] = query_part
            else:
                turned[:, part] += query_part
    grad_query_ref[...] = turned[...].T.astype(jnp.bfloat16)
    grad_keys_ref[...] = keys_sum[...].astype(jnp.bfloat16)
    grad_values_ref[...] = values_sum[...].astype(jnp.bfloat16)


def pair_specs(rows):
    wide = pl.BlockSpec((rows, PAIR), lambda i, spans: (0, i))
    total = pl.BlockSpec((1, 2, rows), lambda i, spans: (i, 0, 0))
    return (wide, total)


def attend_forward(spans, query, keys, values):
    rows, width = query.shape
    pairs = width // PAIR
    wide, total = pair_specs(rows)
    return pl.pallas_call(
        attend_forward_kernel,
        out_shape=(
            jax.ShapeDtypeStruct((rows, width), jnp.bfloat16),
            jax.ShapeDtypeStruct((pairs, 2, rows), jnp.float32),
        ),
        grid_spec=pltpu.PrefetchScalarGridSpec(
            num_scalar_prefetch=1,
            grid=(pairs,),
            in_specs=[wide, wide, wide],
            out_specs=(wide, total),
            scratch_shapes=[pltpu.VMEM((PAIR, rows), jnp.float32)],
        ),
        name="attend_forward",
    )(spans, query, keys, values)


def attend_backward(spans, query, keys, values, context, grad_context, log_total):
    rows, width = query.shape
    pairs = width // PAIR
    wide, total = pair_specs(rows)
    shape = jax.ShapeDtypeStruct((rows, width), jnp.bfloat16)
    return pl.pallas_call(
        attend_backward_kernel,
        out_shape=(shape, shape, shape),
        grid_spec=pltpu.PrefetchScalarGridSpec(
            num_scalar_prefetch=1,
            grid=(pairs,),
            in_specs=[wide, wide, wide, wide, wide, total],
            out_specs=(wide, wide, wide),
            scratch_shapes=[
                pltpu.VMEM((PAIR, rows), jnp.float32),
                pltpu.VMEM((rows, PAIR), jnp.float32),
                pltpu.VMEM((rows, PAIR), jnp.float32),
            ],
        ),
        name="attend_backward",
    )(spans, query, keys, values, context, grad_context, log_total)


AXES = ("rows", "heads")


def exchange(values, bit, devices):
    return lax.ppermute(values, AXES, [(i, i ^ bit) for i in range(devices)])


def my_bit(bit):
    return (lax.axis_index(AXES) & bit) != 0


def gather_doubling(rows, devices):
    share = rows.shape[0]
    rows = rows[None]
    bit = devices // 2
    while bit:
        other = exchange(rows, bit, devices)
        upper = my_bit(bit)
        rows = jnp.concatenate(
            [jnp.where(upper, other, rows), jnp.where(upper, rows, other)], axis=1
        ).reshape(-1, share, D)
        bit = bit // 2
    return rows.reshape(-1, D)


def reduce_halves(values, devices):
    bit = 1
    while bit < devices:
        values = values.reshape(values.shape[0] // 2, 2, *values.shape[1:])
        upper = my_bit(bit)
        keep = jnp.where(upper, values[:, 1], values[:, 0]).astype(jnp.float32)
        sent = jnp.where(upper, values[:, 0], values[:, 1])
        values = (keep + exchange(sent, bit, devices).astype(jnp.float32)).astype(values.dtype)
        bit = bit * 2
    return values[0]


def all_to_all(values):
    return lax.all_to_all(values, AXES, split_axis=0, concat_axis=0, tiled=True)


def pieces_of(rows, devices):
    return rows.reshape(-1, devices, BLOCK_ROWS * D // devices).transpose(1, 0, 2)


def rows_of(pieces):
    return pieces.transpose(1, 0, 2).reshape(-1, D)


def pick_kernel(place_ref, pieces_ref, out_ref):
    blocks, piece = out_ref.shape
    slots = pieces_ref.shape[0]
    chosen = place_ref[...] == lax.broadcasted_iota(jnp.int32, (blocks, slots), 1)
    chosen = jnp.where(chosen, 1.0, 0.0).astype(jnp.bfloat16)
    out_ref[...] = product(chosen, pieces_ref[...])[:, :piece].astype(jnp.bfloat16)


def pick(place, pieces, piece):
    return pl.pallas_call(
        pick_kernel,
        out_shape=jax.ShapeDtypeStruct((place.shape[0], piece), jnp.bfloat16),
        name="pick",
    )(place[:, None], pieces)


def spare_lanes(devices):
    return -(BLOCK_ROWS * D // devices) % PAIR


def route_in(rows, small, place, slots, devices):
    pieces = pieces_of(rows, devices)
    _, capacity, piece = pieces.shape
    spare = spare_lanes(devices)
    deep = -(-small.shape[0] // spare)
    tail = jnp.pad(small, (0, deep * spare - small.shape[0])).reshape(deep, spare)
    tail = jnp.pad(tail, ((0, capacity - deep), (0, 0)))[None]
    tail = jnp.broadcast_to(tail, (devices, capacity, spare))
    moved = all_to_all(jnp.concatenate([pieces, tail], axis=2))
    small_all = moved[:, :deep, piece:].reshape(devices, -1)[:, : small.shape[0]].reshape(-1)
    homed = pick(place, moved.reshape(slots, -1), piece)
    return (all_to_all(homed.reshape(devices, -1, piece)), small_all)


def assemble_kernel(pieces_ref, out_ref, lines, columns):
    devices, slots, _ = pieces_ref.shape
    wide = D // devices
    for row in range(BLOCK_ROWS):
        for piece in range(devices):
            lines[row * slots : (row + 1) * slots, piece * wide : (piece + 1) * wide] = pieces_ref[
                piece, :, row * wide : (row + 1) * wide
            ].astype(jnp.float32)
    for group in range(D // PAIR):
        lanes = slice(group * PAIR, (group + 1) * PAIR)
        for row in range(BLOCK_ROWS):
            columns[group, pl.ds(row, slots, stride=BLOCK_ROWS), :] = lines[
                row * slots : (row + 1) * slots, lanes
            ]
        out_ref[:, lanes] = columns[group]


def assemble(pieces):
    rows = pieces.shape[1] * BLOCK_ROWS
    return pl.pallas_call(
        assemble_kernel,
        out_shape=jax.ShapeDtypeStruct((rows, D), jnp.float32),
        scratch_shapes=[
            pltpu.VMEM((rows, D), jnp.float32),
            pltpu.VMEM((D // PAIR, rows, PAIR), jnp.float32),
        ],
        name="assemble",
    )(pieces)


def place_kernel(wide_ref, narrow_ref, slot_ref, out_ref, turned, lined):
    columns = wide_ref.shape[0]
    slots = out_ref.shape[0]
    blocks = lined.shape[0]
    for group in range(2):
        part = narrow_ref[group * columns : (group + 1) * columns, :]
        turned[group * D : (group + 1) * D, :] = part.astype(jnp.float32).T
    turned[2 * D :, :] = wide_ref[...].astype(jnp.float32).T
    for row in range(BLOCK_ROWS):
        lined[:, row * columns : (row + 1) * columns] = turned[
            pl.ds(row, blocks, stride=BLOCK_ROWS), :
        ]
    chosen = slot_ref[...] == lax.broadcasted_iota(jnp.int32, (slots, blocks), 0)
    chosen = jnp.where(chosen, 1.0, 0.0).astype(jnp.bfloat16)
    out_ref[...] = product(chosen, lined[...].astype(jnp.bfloat16)).astype(jnp.bfloat16)


def route_out(wide, narrow, slot, slots, devices):
    columns = wide.shape[0]
    blocks = slot.shape[0]
    slotted = pl.pallas_call(
        place_kernel,
        out_shape=jax.ShapeDtypeStruct((slots, BLOCK_ROWS * columns), jnp.bfloat16),
        scratch_shapes=[
            pltpu.VMEM((blocks * BLOCK_ROWS, columns), jnp.float32),
            pltpu.VMEM((blocks, BLOCK_ROWS * columns), jnp.float32),
        ],
        name="place",
    )(wide, narrow, slot[None, :])
    return assemble(all_to_all(slotted.reshape(devices, -1, BLOCK_ROWS * columns)))


KEY_BLOCKS = D // BLOCK_ROWS


def even_homes(blocks, capacity, small_share, devices):
    fits = spare_lanes(devices) * capacity >= small_share
    return fits and KEY_BLOCKS % devices == 0 and (blocks - 2 * KEY_BLOCKS) % devices == 0


def gather_rows(weights, small, slot, devices):
    slots = devices * (weights.shape[0] // BLOCK_ROWS)
    low = weights.astype(jnp.bfloat16)
    small = small.astype(jnp.bfloat16)
    if not even_homes(slot.shape[0], slots // devices, small.shape[0], devices):
        rows = unpack_rows(lax.all_gather(low, AXES, axis=0, tiled=True), slot)
        return (rows, lax.all_gather(small, AXES, axis=0, tiled=True))
    place = jnp.concatenate(
        [slot[KEY_BLOCKS:].reshape(devices, -1), slot[:KEY_BLOCKS].reshape(devices, -1)], axis=1
    ).reshape(-1)
    homed, small_all = route_in(low, small, place, slots, devices)
    split = homed.shape[1] - KEY_BLOCKS // devices
    rest = lax.all_gather(rows_of(homed[:, :split]), AXES, axis=0, tiled=True)
    keys = gather_doubling(rows_of(homed[:, split:]), devices)
    return ((keys, rest[:D], rest[D : D + FF], rest[D + FF :]), small_all)


def weight_grads_kernel(pre_ref, hidden_ref, active_ref, branch_ref, out_ref, turned):
    step = pl.program_id(0)
    half = pl.num_programs(0) // 2

    @pl.when(step == 0)
    def _():
        turned[...] = hidden_ref[...].T

    @pl.when(step == half)
    def _():
        turned[...] = branch_ref[...].T

    @pl.when(step < half)
    def _():
        out_ref[...] = product(turned[...], pre_ref[...]).astype(jnp.bfloat16)

    @pl.when(step >= half)
    def _():
        out_ref[...] = product(turned[...], active_ref[...]).astype(jnp.bfloat16)


def weight_grads(grad_pre, hidden_low, active, grad_branch):
    rows = grad_pre.shape[0]
    width = 1024
    half = FF // width
    whole = pl.BlockSpec((rows, D), lambda i: (0, 0))
    return pl.pallas_call(
        weight_grads_kernel,
        out_shape=jax.ShapeDtypeStruct((D, 2 * FF), jnp.bfloat16),
        grid=(2 * half,),
        in_specs=[
            pl.BlockSpec((rows, width), lambda i: (0, jnp.minimum(i, half - 1))),
            whole,
            pl.BlockSpec((rows, width), lambda i: (0, jnp.maximum(i - half, 0))),
            whole,
        ],
        out_specs=pl.BlockSpec((D, width), lambda i: (0, i)),
        scratch_shapes=[pltpu.VMEM((D, rows), jnp.bfloat16)],
        name="weight_grads",
    )(grad_pre, hidden_low, active, grad_branch)


def scatter_grads(grad_key, grad_out, grad_wide, small_grad, slot, slots, devices):
    blocks = slot.shape[0]
    if not even_homes(blocks, slots // devices, small_grad.shape[0] // devices, devices):
        rows = jnp.concatenate([grad_key, grad_out, grad_wide], axis=1).T
        rows = rows.reshape(blocks, BLOCK_ROWS * D)
        chosen = slot[:, None] == jnp.arange(slots, dtype=jnp.int32)[None, :]
        slotted = inner_rows(chosen.astype(jnp.bfloat16), rows).astype(jnp.bfloat16)
        return (
            lax.psum_scatter(slotted.reshape(-1, D), AXES, scatter_dimension=0, tiled=True),
            lax.psum_scatter(small_grad, AXES, scatter_dimension=0, tiled=True),
        )
    wide_part = lax.psum_scatter(grad_wide, AXES, scatter_dimension=0, tiled=True)
    share = D // devices
    small_share = small_grad.shape[0] // devices
    small_deep = -(-small_share // D)
    deep = -(-(2 * share + small_deep) // 8) * 8 - 2 * share
    small_rows = jnp.pad(
        small_grad.reshape(devices, small_share).astype(jnp.bfloat16),
        ((0, 0), (0, deep * D - small_share)),
    ).reshape(devices, deep, D)
    packed = jnp.concatenate(
        [grad_key.reshape(devices, share, D), grad_out.reshape(devices, share, D), small_rows],
        axis=1,
    )
    summed = reduce_halves(packed, devices)
    small_part = summed[2 * share : 2 * share + small_deep].reshape(-1)[:small_share]
    return (route_out(wide_part, summed, slot, slots, devices), small_part.astype(jnp.float32))


def adamw_update(master, first, second, grad, decay, rate):
    correct = 1.0 - 0.5**STEP
    first_new = 0.5 * first + 0.5 * grad
    second_new = 0.5 * second + 0.5 * grad * grad
    update = first_new / correct / (jnp.sqrt(second_new / correct) + 1e-08) + decay * master
    return (master - rate * update, first_new, second_new)


def body(
    hidden_in,
    cotangent,
    part_lengths,
    segment_start,
    query_weight,
    value_weight,
    shared_down,
    shared_up,
    owner,
    weights,
    first_moment,
    second_moment,
    small_weights,
    small_first,
    small_second,
):
    capacity = weights.shape[0] // BLOCK_ROWS
    devices = lax.axis_size("rows") * lax.axis_size("heads")
    slot = slot_index(owner, capacity)
    (key_rows, out_rows, up_rows, down_rows), small_all = gather_rows(
        weights, small_weights, slot, devices
    )
    (
        scale_q_rank,
        scale_v_rank,
        scale_q_out,
        scale_v_out,
        out_bias,
        up_bias,
        down_bias,
        gain_one,
        shift_one,
        gain_two,
        shift_two,
    ) = [piece.astype(jnp.float32) for piece in split_small(small_all)]
    projected = product(hidden_in, shared_down).astype(jnp.bfloat16)
    projected_wide = projected.astype(jnp.float32)
    rank_q = (scale_q_rank * projected_wide).astype(jnp.bfloat16)
    rank_v = (scale_v_rank * projected_wide).astype(jnp.bfloat16)
    side_q = product(rank_q, shared_up)
    side_v = product(rank_v, shared_up)
    query = (product(hidden_in, query_weight) + scale_q_out * side_q).astype(jnp.bfloat16)
    keys = product(hidden_in, key_rows).astype(jnp.bfloat16)
    values = (product(hidden_in, value_weight) + scale_v_out * side_v).astype(jnp.bfloat16)
    mine = lax.axis_index("heads")
    spans = jnp.concatenate([part_lengths[mine], segment_start[mine][None]])
    context, log_total = attend_forward(spans, query, keys, values)
    attended = product(context, out_rows) + out_bias
    first_sum = hidden_in.astype(jnp.float32) + attended
    norm_one, inverse_one = normalize(first_sum)
    hidden_one = norm_one * gain_one + shift_one
    hidden_low = hidden_one.astype(jnp.bfloat16)
    pre_act = product_t(hidden_low, up_rows) + up_bias
    share = 0.5 * (1.0 + lax.erf(pre_act * 0.7071067811865476))
    slope = share + pre_act * jnp.exp(-0.5 * pre_act * pre_act) * 0.3989422804014327
    active, slope = lax.optimization_barrier(
        ((pre_act * share).astype(jnp.bfloat16), slope.astype(jnp.bfloat16))
    )
    second_sum = hidden_one + product(active, down_rows) + down_bias
    norm_two, inverse_two = normalize(second_sum)
    block_out = (norm_two * gain_two + shift_two).astype(jnp.bfloat16)
    grad_top = cotangent.astype(jnp.float32)
    grad_gain_two = jnp.sum(grad_top * norm_two, axis=0)
    grad_shift_two = jnp.sum(grad_top, axis=0)
    grad_second = norm_back(grad_top * gain_two, norm_two, inverse_two)
    grad_branch = grad_second.astype(jnp.bfloat16)
    grad_down_bias = jnp.sum(grad_branch.astype(jnp.float32), axis=0)
    grad_pre = (product_t(grad_branch, down_rows) * slope.astype(jnp.float32)).astype(jnp.bfloat16)
    grad_up_bias = jnp.sum(grad_pre.astype(jnp.float32), axis=0)
    grad_wide = weight_grads(grad_pre, hidden_low, active, grad_branch)
    grad_hidden = grad_second + product(grad_pre, up_rows)
    grad_gain_one = jnp.sum(grad_hidden * norm_one, axis=0)
    grad_shift_one = jnp.sum(grad_hidden, axis=0)
    grad_first = norm_back(grad_hidden * gain_one, norm_one, inverse_one)
    grad_attended = grad_first.astype(jnp.bfloat16)
    grad_out_bias = jnp.sum(grad_attended.astype(jnp.float32), axis=0)
    grad_out = inner_rows(grad_attended, context).astype(jnp.bfloat16)
    grad_context = product_t(grad_attended, out_rows).astype(jnp.bfloat16)
    grad_query, grad_keys, grad_values = attend_backward(
        spans, query, keys, values, context, grad_context, log_total
    )
    grad_key = inner_rows(grad_keys, hidden_in).astype(jnp.bfloat16)
    grad_query_wide = grad_query.astype(jnp.float32)
    grad_values_wide = grad_values.astype(jnp.float32)
    grad_scale_q_out = jnp.sum(grad_query_wide * side_q, axis=0)
    grad_scale_v_out = jnp.sum(grad_values_wide * side_v, axis=0)
    grad_side_q = (scale_q_out * grad_query_wide).astype(jnp.bfloat16)
    grad_side_v = (scale_v_out * grad_values_wide).astype(jnp.bfloat16)
    grad_rank_q = product_t(grad_side_q, shared_up)
    grad_rank_v = product_t(grad_side_v, shared_up)
    grad_scale_q_rank = jnp.sum(grad_rank_q * projected_wide, axis=0)
    grad_scale_v_rank = jnp.sum(grad_rank_v * projected_wide, axis=0)
    grad_projected = (grad_rank_q * scale_q_rank + grad_rank_v * scale_v_rank).astype(jnp.bfloat16)
    grad_input = grad_first + product_t(grad_query, query_weight) + product_t(grad_keys, key_rows)
    grad_input = (
        grad_input + product_t(grad_values, value_weight) + product_t(grad_projected, shared_down)
    )
    input_grad = grad_input.astype(jnp.bfloat16)
    small_grad = jnp.concatenate(
        [
            grad_scale_q_rank,
            grad_scale_v_rank,
            grad_scale_q_out,
            grad_scale_v_out,
            grad_out_bias,
            grad_up_bias,
            grad_down_bias,
            grad_gain_one,
            grad_shift_one,
            grad_gain_two,
            grad_shift_two,
        ]
    )
    owned_grad, owned_small = scatter_grads(
        grad_key, grad_out, grad_wide, small_grad, slot, devices * capacity, devices
    )
    new_weights, new_first, new_second = adamw_update(
        weights, first_moment, second_moment, owned_grad, 0.01, 0.03
    )
    new_small, new_small_first, new_small_second = adamw_update(
        small_weights, small_first, small_second, owned_small, 0.0, 0.3
    )
    return (
        block_out,
        input_grad,
        new_weights,
        new_first,
        new_second,
        new_weights.astype(jnp.bfloat16),
        new_small,
        new_small_first,
        new_small_second,
        new_small.astype(jnp.bfloat16),
    )


def solution(mesh):
    return jax.shard_map(
        body,
        mesh=mesh,
        in_specs=(
            P(("rows", "heads"), None),
            P(("rows", "heads"), None),
            P("rows", None),
            P("rows"),
            P(),
            P(),
            P(),
            P(),
            P(),
            P(("rows", "heads"), None),
            P(("rows", "heads"), None),
            P(("rows", "heads"), None),
            P(("rows", "heads")),
            P(("rows", "heads")),
            P(("rows", "heads")),
        ),
        out_specs=(
            P(("rows", "heads"), None),
            P(("rows", "heads"), None),
            P(("rows", "heads"), None),
            P(("rows", "heads"), None),
            P(("rows", "heads"), None),
            P(("rows", "heads"), None),
            P(("rows", "heads")),
            P(("rows", "heads")),
            P(("rows", "heads")),
            P(("rows", "heads")),
        ),
        check_vma=False,
    )
```
